128 devices in a mesh: grp: 4 (over z), slab: 32 (over x, y, core).
Axes of the slice: x: 4, y: 4, z: 4, core: 2. Of those that a mesh axis runs over, the one named last changes fastest.
Arguments:
- probes: float32 [64, 512, 8, 512], P(None, 'slab', None, 'grp'), may hold values from -6 to 6
- courant: float32 [512, 8, 512], P('slab', None, 'grp'), may hold values from 0.02 to 0.18
- rec_cell: int32 [8192], P(('grp', 'slab')), may hold values from 0 to 16383
- rec_owner: int32 [8192, 1], P(('grp', 'slab')), may hold values from 0 to 31; in each aligned block of 64 rows (0 to 63, 64 to 127, ...) at most 8 rows name the same one
- trace_weight: float32 [8192], P(('grp', 'slab')), may hold values from 1 to 10
Outputs:
- wavefield: float32 [64, 512, 8, 512], P(None, 'slab', None, 'grp')
- q_basis: float32 [32768, 256], P(('grp', 'slab'))
- r_factor: float32 [64, 64], replicated
The draws below stay inside these ranges and needn't reach their ends.
Inputs may be any that keep to these rules, and one draw needn't show every extreme that they name: `rec_owner`: among the receivers of one device no owner is named by more than 8; in every draw some device names some owner exactly 8 times.
All inputs are finite; a program needn't handle non-finite values.
Results may differ from the reference program's by a relative error of at most 0.00016.
Values sent between devices are 32-bit elements; how exact they have to be, the bound alone decides.
A program may use at most 192 MiB of HBM per device.

```python
import math
import jax
import jax.numpy as jnp
import numpy as np
from jax import lax

PROBES = 64
CX = 16
CY = 8
CZ = 128
STEPS = 4
REC_DEV = 64
CAP = 8
NX = 512
NY = 8
NZ = 512
RECEIVERS = 8192
SLOTS = 32768
N_GRP = 4
N_SLAB = 32


def place_ends(result, own_key, low, high):
    longest = result.shape.index(max(result.shape))
    spots = []
    for shift in (0, 1):
        where = [jax.random.randint(jax.random.fold_in(own_key, axis), (), 0, length) for axis, length in enumerate(result.shape)]
        where[longest] = (where[longest] + shift) % result.shape[longest]
        spots.append(tuple(where))
    return result.at[spots[0]].set(low).at[spots[1]].set(high)


def steps_of(key, shape, shards, low, top_value):
    def one(position, blocks):
        heights = jax.random.uniform(jax.random.fold_in(jax.random.fold_in(key, 6), position), (blocks,), jnp.float32, low / len(shards), top_value / len(shards))
        return jnp.repeat(jnp.exp(heights), shape[position] // blocks).reshape((-1,) + (1,) * (len(shape) - position - 1))

    loudness = one(*shards[0])
    for cut in shards[1:]:
        loudness = loudness * one(*cut)
    return loudness


def routed_block(key, own, number, rows, amount, top, bound, slope):
    ranking = jax.random.permutation(key, amount)
    heavy_load, usual = load_shares(amount, rows * top, bound, slope, True), load_shares(amount, rows * top, bound, slope, False)
    places = jnp.arange(amount)

    def named(lengths, rotation):
        used = int((lengths > 0).sum())
        fixed = max(1, used // 4)
        passed = fixed + (places - fixed + rotation * (used - fixed)) % max(1, amount - fixed)
        return jnp.zeros((amount,), jnp.int32).at[ranking[jnp.where(places < fixed, places, passed)]].set(jnp.asarray(lengths, jnp.int32))

    lengths = jnp.where(number % 4 == 0, named(heavy_load, number // 4), named(usual, number - number // 4 - 1))
    mixed = jax.random.permutation(jax.random.fold_in(own, 3), amount)
    giver, receiver = mixed[0:amount // 2 * 2:2], mixed[1:amount // 2 * 2:2]
    slack = jnp.minimum(lengths[giver] - 1, bound - lengths[receiver]) // 2
    slack = jnp.where((giver == ranking[0]) | (receiver == ranking[0]) | (lengths[receiver] == 0), 0, jnp.maximum(slack, 0))
    passed = jax.random.randint(jax.random.fold_in(own, 4), (amount // 2,), 0, 1 << 20) % (slack + 1)
    lengths = lengths.at[giver].add(-passed).at[receiver].add(passed)
    items = jnp.searchsorted(jnp.cumsum(lengths), jnp.arange(rows * top), side="right").astype(jnp.int32)
    table = items.reshape(top, rows).T
    table = table[jax.random.permutation(jax.random.fold_in(own, 1), rows)]
    rotation = jax.random.randint(jax.random.fold_in(own, 2), (rows, 1), 0, top)
    return jnp.take_along_axis(table, (jnp.arange(top)[None, :] + rotation) % top, axis=1)


def load_shares(amount, total, limit, skew, full):
    weights = [(1 << 20) // math.isqrt(rank ** skew) + 1 for rank in range(1, amount + 1)]
    largest = limit if full else min(limit, max(-(-total // amount), total * weights[0] // sum(weights)))
    least = 1 if total - largest >= amount - 1 else 0
    counts, spare = [largest] + [least] * (amount - 1), total - largest - least * (amount - 1)
    while spare > 0:
        movable = [i for i in range(1, amount) if counts[i] < largest] or [i for i in range(1, amount) if counts[i] < limit]
        mass, remaining = sum([weights[i] for i in movable]), spare
        for i in movable:
            extra = min(limit - counts[i], max(1, remaining * weights[i] // mass), spare)
            counts[i] = counts[i] + extra
            spare = spare - extra
    return np.array(counts)


def normal_values(stream_key, extent, scale, bound, pieces=(), kind=jnp.bfloat16):
    array = jax.random.normal(stream_key, extent, jnp.float32) * scale
    if len(pieces) > 0:
        array = steps_of(stream_key, extent, pieces, -0.22, 0.18) * array
    return jnp.clip(array, min=-bound, max=bound).astype(kind)


def setup_inputs(seed: int = 0) -> dict:
    keys = jax.random.split(jax.random.key(seed), 6)
    probes = normal_values(keys[0], (PROBES, NX, NY, NZ), 1.0, 6.0, ((1, 32), (3, 4)), jnp.float32)
    courant = jnp.clip(jnp.exp(math.log(0.18) - 2.1972246 * jax.random.uniform(keys[1], (NX, NY, NZ), jnp.float32) ** steps_of(keys[1], (NX, NY, NZ), ((0, 32), (2, 4)), -0.2, 0.2)), 0.02, 0.18)
    rec_cell = place_ends(jax.random.randint(keys[2], (RECEIVERS,), 0, CX * CY * CZ), jax.random.fold_in(keys[2], 1), 0, (CX * CY * CZ) - 1).astype(jnp.int32)
    rec_owner_keys = jax.random.split(jax.random.fold_in(keys[3], 1), RECEIVERS // REC_DEV)
    rec_owner_turns = jax.random.permutation(jax.random.fold_in(keys[3], 3), RECEIVERS // REC_DEV)
    rec_owner = jax.vmap(lambda own, number: routed_block(jax.random.fold_in(keys[3], 2), own, number, REC_DEV, N_SLAB, 1, CAP, 2))(rec_owner_keys, rec_owner_turns).reshape((RECEIVERS, 1))
    trace_weight = jnp.clip(jnp.exp(math.log(10.0) - 2.3025851 * jax.random.uniform(keys[4], (RECEIVERS,), jnp.float32) ** steps_of(keys[4], (RECEIVERS,), ((0, 128),), -0.2, 0.2)), 1.0, 10.0)
    return {"probes": probes, "courant": courant, "rec_cell": rec_cell, "rec_owner": rec_owner, "trace_weight": trace_weight}


stencil_weights = (-205.0 / 72.0, 8.0 / 5.0, -1.0 / 5.0, 8.0 / 315.0, -1.0 / 560.0)

def laplace(padded):
    size_x = padded.shape[1] - 8
    size_y = padded.shape[2] - 8
    size_z = padded.shape[3] - 8
    center = padded[:, 4:4 + size_x, 4:4 + size_y, 4:4 + size_z]
    total = 3.0 * stencil_weights[0] * center
    for offset in range(1, 5):
        beside_all = padded[:, 4 + offset:4 + offset + size_x, 4:4 + size_y, 4:4 + size_z]
        beside_all = beside_all + padded[:, 4 - offset:4 - offset + size_x, 4:4 + size_y, 4:4 + size_z]
        beside_all = beside_all + padded[:, 4:4 + size_x, 4 + offset:4 + offset + size_y, 4:4 + size_z]
        beside_all = beside_all + padded[:, 4:4 + size_x, 4 - offset:4 - offset + size_y, 4:4 + size_z]
        beside_all = beside_all + padded[:, 4:4 + size_x, 4:4 + size_y, 4 + offset:4 + offset + size_z]
        beside_all = beside_all + padded[:, 4:4 + size_x, 4:4 + size_y, 4 - offset:4 - offset + size_z]
        total = total + stencil_weights[offset] * beside_all
    return total

def reference(probes, courant, rec_cell, rec_owner, trace_weight):
    device = jnp.arange(RECEIVERS, dtype=jnp.int32) // REC_DEV
    group_index = device // N_SLAB
    slab_index = device % N_SLAB
    local_x = rec_cell // (CY * CZ)
    local_y = rec_cell // CZ % CY
    local_z = rec_cell % CZ
    global_x = slab_index * CX + local_x
    global_z = group_index * CZ + local_z
    flat_index = ((global_x * NY + local_y) * NZ + global_z).astype(jnp.int32)
    speed = courant[None]

    def propagate(field):
        previous = field[None]
        current = field[None]
        samples = []
        for moment in range(STEPS):
            padded = jnp.pad(current, ((0, 0), (4, 4), (4, 4), (4, 4)))
            advanced = 2.0 * current - previous + speed * laplace(padded)
            previous = current
            current = advanced
            samples.append(current.reshape(-1)[flat_index])
        return (current[0], jnp.stack(samples))
    final, traces = lax.map(propagate, probes)
    rows = jnp.transpose(traces, (2, 1, 0)) * trace_weight[:, None, None]
    rows = rows.reshape(RECEIVERS, STEPS * PROBES)
    sketch = rows.reshape(RECEIVERS * STEPS, PROBES)
    gram = jnp.dot(sketch.T.astype(jnp.float32), sketch.astype(jnp.float32), preferred_element_type=jnp.float32, precision=lax.Precision.HIGHEST)
    lower = jnp.linalg.cholesky(gram)
    row_count = RECEIVERS * STEPS
    r_factor = lower.T / math.sqrt(row_count)
    owners = rec_owner[:, 0].reshape(N_GRP * N_SLAB, REC_DEV)
    hits = (owners[:, :, None] == jnp.arange(N_SLAB, dtype=jnp.int32)[None, None, :]).astype(jnp.int32)
    before = jnp.cumsum(hits, axis=1) - hits
    slots = lax.optimization_barrier(jnp.sum(before * hits, axis=2)).reshape(RECEIVERS)
    owner_flat = rec_owner[:, 0]
    target = ((group_index * N_SLAB + owner_flat) * N_SLAB + slab_index) * CAP + slots
    placed = jnp.zeros((SLOTS, STEPS * PROBES), jnp.float32).at[target.astype(jnp.int32)].set(rows)
    solved = jax.scipy.linalg.solve_triangular(lower, placed.reshape(SLOTS * STEPS, PROBES).T, lower=True)
    q_basis = (solved.T * math.sqrt(row_count)).reshape(SLOTS, STEPS * PROBES)
    return (final, q_basis, r_factor)
```

```python
import functools
import math

import jax
import jax.numpy as jnp
from jax import lax
from jax.experimental import pallas as pl
from jax.experimental.pallas import tpu as pltpu
from jax.sharding import PartitionSpec as P

PROBES = 64
CX = 16
CY = 8
CZ = 128
STEPS = 4
CHUNK = 8
CHUNKS = PROBES // CHUNK
GROUP = 4
WIDTH = 4
CAP = 8
MESH = pl.DeviceIdType.MESH
EXACT = lax.Precision.HIGHEST

A0 = -205.0 / 72.0
A = (0.0, 8.0 / 5.0, -1.0 / 5.0, 8.0 / 315.0, -1.0 / 560.0)


def dot_nt(a, b):
    return lax.dot_general(
        a, b, (((1,), (1,)), ((), ())), precision=EXACT, preferred_element_type=jnp.float32
    )


def kernel(
    n_grp,
    n_slab,
    probes,
    courant,
    cell,
    owner,
    weight,
    wave_out,
    q_out,
    r_out,
    stage,
    first_halo,
    field,
    latest,
    speed,
    z_own,
    z_halo,
    z_fix,
    z_map,
    traces,
    outgoing,
    incoming,
    sum_a,
    sum_b,
    sum_c,
    load_sem,
    store_sem,
    x_send,
    x_recv,
    z_send,
    z_recv,
    a2a_send,
    a2a_recv,
    own_sem,
    sum_send,
    sum_recv,
):
    s = lax.axis_index("slab")
    g = lax.axis_index("grp")
    has = ((s > 0, s < n_slab - 1), (g > 0, g < n_grp - 1))

    def load(c):
        return pltpu.make_async_copy(
            probes.at[pl.ds(c * CHUNK, CHUNK)], stage.at[c], load_sem.at[c]
        )

    for c in range(CHUNKS):
        load(c).start()

    barrier = pltpu.get_barrier_semaphore()

    @pl.loop(1, n_slab)
    def _(k):
        pl.semaphore_signal(
            barrier, inc=1, device_id={"slab": lax.rem(s + k, n_slab)}, device_id_type=MESH
        )

    @pl.loop(1, n_grp)
    def _(k):
        pl.semaphore_signal(
            barrier, inc=1, device_id={"grp": lax.rem(g + k, n_grp)}, device_id_type=MESH
        )

    lane = lax.broadcasted_iota(jnp.int32, (8, 128), 1)
    edge = (lane < WIDTH) | (lane >= CZ - WIDTH)
    lane_slot = lane // 8
    low_half = (lane % 8) < WIDTH

    row_i = lax.broadcasted_iota(jnp.int32, (128, 128), 0)
    col_i = lax.broadcasted_iota(jnp.int32, (128, 128), 1)
    gap = jnp.abs(row_i - col_i)
    crossing = (row_i // 8 == col_i // 8) & ((row_i % 8 < WIDTH) != (col_i % 8 < WIDTH))
    table = jnp.zeros((128, 128), jnp.float32)
    for k in range(1, 5):
        table = jnp.where(gap == k, A[k], table)
    z_map[...] = jnp.where(crossing, table, 0.0)

    @pl.loop(0, CX)
    def _(x):
        for y in range(CY):
            speed[x, y] = jnp.broadcast_to(courant[x, pl.ds(y, 1), :], (8, 128))

    blank = jnp.zeros((WIDTH, CY, 8, 128), jnp.float32)
    for side in range(2):

        @pl.when(jnp.logical_not(has[0][side]))
        def _(side=side):
            @pl.loop(0, STEPS)
            def _(t):
                @pl.loop(0, CHUNKS)
                def _(c):
                    field[t, c, pl.ds(side * (CX + WIDTH), WIDTH)] = blank

        @pl.when(jnp.logical_not(has[1][side]))
        def _(side=side):
            @pl.loop(0, STEPS)
            def _(t):
                @pl.loop(0, CHUNKS)
                def _(c):
                    z_halo[side, t, c] = jnp.zeros((8, 8, 128), jnp.float32)

    def x_first(c, way):
        return pltpu.make_async_remote_copy(
            src_ref=probes.at[pl.ds(c * CHUNK, CHUNK), pl.ds((1 - way) * (CX - WIDTH) * CY, WIDTH * CY)],
            dst_ref=first_halo.at[way, c],
            send_sem=x_send.at[way, c],
            recv_sem=x_recv.at[way, 0, c],
            device_id={"slab": s + 1 - 2 * way},
            device_id_type=MESH,
        )

    def x_copy(t, c, way):
        return pltpu.make_async_remote_copy(
            src_ref=field.at[t, c, pl.ds(WIDTH + (1 - way) * (CX - WIDTH), WIDTH)],
            dst_ref=field.at[t, c, pl.ds(way * (CX + WIDTH), WIDTH)],
            send_sem=x_send.at[way, c],
            recv_sem=x_recv.at[way, t, c],
            device_id={"slab": s + 1 - 2 * way},
            device_id_type=MESH,
        )

    def z_copy(t, c, way):
        return pltpu.make_async_remote_copy(
            src_ref=z_own.at[t, c],
            dst_ref=z_halo.at[way, t, c],
            send_sem=z_send.at[way, c],
            recv_sem=z_recv.at[way, t, c],
            device_id={"grp": g + 1 - 2 * way},
            device_id_type=MESH,
        )

    def sending(axis, way):
        return has[axis][1 - way]

    def receiving(axis, way):
        return has[axis][way]

    pl.semaphore_wait(barrier, n_slab - 1 + n_grp - 1)

    def send_first(c):
        for way in range(2):

            @pl.when(sending(0, way))
            def _(way=way):
                x_first(c, way).start()

    for c in range(GROUP):
        send_first(c)

    def pack(values):
        packed = jnp.zeros((8, 128), jnp.float32)
        for i, value in enumerate(values):
            packed = jnp.where(
                lane_slot == i, pltpu.roll(value, (4 + 8 * i) % 128, 1), packed
            )
        return packed

    stage_rows = stage.reshape(CHUNKS * CHUNK * CX * CY, CZ)
    halo_rows = first_halo.reshape(2 * CHUNKS * CHUNK * WIDTH * CY, CZ)

    def bring_in(c):
        load(c).wait()

        @pl.loop(0, CX // 2)
        def _(j):
            values = []
            for i in range(16):
                value = stage_rows[pl.ds(c * 1024 + j * 16 + i, 8, stride=CX * CY), :]
                field[0, c, WIDTH + 2 * j + i // 8, i % 8] = value
                values.append(value)
            z_own[0, c, j] = pack(values)

        for way in range(2):

            @pl.when(sending(1, way))
            def _(way=way):
                z_copy(0, c, way).start()

    @pl.loop(0, GROUP)
    def _(c):
        bring_in(c)

    weights = weight[...]

    def advance(c, t):
        for way in range(2):

            @pl.when(receiving(0, way))
            def _(way=way):
                @pl.when(t == 0)
                def _():
                    x_first(c, way).wait_recv()

                    @pl.loop(0, WIDTH)
                    def _(x):
                        for y in range(CY):
                            field[0, c, way * (CX + WIDTH) + x, y] = halo_rows[
                                pl.ds((way * CHUNKS + c) * 256 + x * 8 + y, 8, stride=WIDTH * CY), :
                            ]

                @pl.when(t > 0)
                def _():
                    x_copy(t, c, way).wait_recv()

            @pl.when(receiving(1, way))
            def _(way=way):
                z_copy(t, c, way).wait_recv()

        mine = z_own[t, c].reshape(64, 128)
        left = z_halo[0, t, c].reshape(64, 128)
        right = z_halo[1, t, c].reshape(64, 128)
        half = lax.broadcasted_iota(jnp.int32, (64, 128), 1) % 8 < WIDTH
        change = jnp.where(half, left, right) - mine
        z_fix[...] = lax.dot_general(
            change, z_map[...], (((1,), (0,)), ((), ())), precision=EXACT,
            preferred_element_type=jnp.float32,
        ).reshape(8, 8, 128)
        before = jnp.maximum(t - 1, 0)

        @pl.loop(0, CX // 2)
        def _(j):
            fix = z_fix[j]
            values = []
            for i in range(16):
                y = i % 8
                x = 2 * j + i // 8

                def at(dx, dy):
                    return field[t, c, WIDTH + x + dx, y + dy]

                center = at(0, 0)
                total = (3.0 * A0) * center
                for k in range(1, 5):
                    beside = at(k, 0) + at(-k, 0)
                    if y + k < CY:
                        beside = beside + at(0, k)
                    if y - k >= 0:
                        beside = beside + at(0, -k)
                    beside = beside + (pltpu.roll(center, k, 1) + pltpu.roll(center, CZ - k, 1))
                    total = total + A[k] * beside
                correction = pltpu.roll(fix, (128 - 4 - 8 * i) % 128, 1)
                total = total + jnp.where(edge, correction, 0.0)
                old = field[before, c, WIDTH + x, y]
                value = (2.0 * center - old) + speed[x, y] * total
                field[t + 1, c, WIDTH + x, y] = value
                latest[16 * j + i] = value
                values.append(value)

            @pl.when(t < STEPS - 1)
            def _():
                z_own[t + 1, c, j] = pack(values)

        @pl.when(t < STEPS - 1)
        def _():
            for way in range(2):

                @pl.when(sending(0, way))
                def _(way=way):
                    @pl.when(t == 0)
                    def _():
                        x_first(c, way).wait_send()

                    @pl.when(t > 0)
                    def _():
                        x_copy(t, c, way).wait_send()

                    x_copy(t + 1, c, way).start()

                @pl.when(sending(1, way))
                def _(way=way):
                    z_copy(t, c, way).wait_send()
                    z_copy(t + 1, c, way).start()

        @pl.when(t == STEPS - 1)
        def _():
            for way in range(2):

                @pl.when(sending(0, way))
                def _(way=way):
                    x_copy(t, c, way).wait_send()

                @pl.when(sending(1, way))
                def _(way=way):
                    z_copy(t, c, way).wait_send()

        found = jnp.zeros((8, 128), jnp.float32)
        for r in range(cell.shape[0]):
            where = cell[r]
            value = latest[where // CZ]
            shift = (r + CZ) - where % CZ
            value = pltpu.roll(value, shift % 128, 1)
            found = jnp.where(lane == r, value, found)
        traces[t, pl.ds(c * CHUNK, CHUNK), :] = found * weights

        @pl.when(t == STEPS - 1)
        def _():
            @pl.loop(0, CX)
            def _(x):
                for y in range(CY):
                    stage_rows[pl.ds(c * 1024 + x * 8 + y, 8, stride=CX * CY), :] = latest[x * 8 + y]

            pltpu.make_async_copy(
                stage.at[c], wave_out.at[pl.ds(c * CHUNK, CHUNK)], store_sem.at[c]
            ).start()

    @pl.loop(0, CHUNKS * STEPS)
    def _(n):
        block = n // (GROUP * STEPS)
        t = n % (GROUP * STEPS) // GROUP
        c = block * GROUP + n % GROUP
        advance(c, t)

        @pl.when((t == STEPS - 1) & (block < CHUNKS // GROUP - 1))
        def _():
            send_first(c + GROUP)
            bring_in(c + GROUP)

    gram = jnp.zeros((PROBES, PROBES), jnp.float32)
    for t in range(STEPS):
        gram = gram + dot_nt(traces[t], traces[t])
    folded = jnp.concatenate([gram[:32], gram[32:]], axis=1)

    n_y = 8
    place_y = s % n_y
    place_x = s // n_y

    def stage_copies(buffer, count, me, base, device):
        def one(k):
            return pltpu.make_async_remote_copy(
                src_ref=buffer.at[me],
                dst_ref=buffer.at[me],
                send_sem=sum_send.at[base + k],
                recv_sem=sum_recv.at[base + k],
                device_id=device(lax.rem(me + k, count)),
                device_id_type=MESH,
            )

        return [one(k) for k in range(1, count)]

    def begin(buffer, count, me, base, device, value):
        buffer[me] = value
        copies = stage_copies(buffer, count, me, base, device)
        for copy in copies:
            copy.start()
        return copies

    def finish(buffer, count, copies):
        for copy in copies:
            copy.wait_recv()
        total = buffer[0]
        for k in range(1, count):
            total = total + buffer[k]
        for copy in copies:
            copy.wait_send()
        return total

    n_x = n_slab // n_y
    copies = begin(
        sum_a, n_y, place_y, 0, lambda other: {"slab": place_x * n_y + other}, folded
    )

    recs = cell.shape[0]
    own_col = owner[...]
    r_row = lax.broadcasted_iota(jnp.int32, (recs, 128), 0)
    r_col = lax.broadcasted_iota(jnp.int32, (recs, 128), 1)
    own_row = jnp.sum(jnp.where(r_row == r_col, own_col, 0), axis=0, keepdims=True)
    same = (own_col == own_row) & (r_row < r_col)
    slot = jnp.sum(jnp.where(same, 1, 0), axis=0, keepdims=True)
    lane_row = lax.broadcasted_iota(jnp.int32, (1, 128), 1)
    target = jnp.where(lane_row < recs, own_row * CAP + slot, -1)
    spots = lax.broadcasted_iota(jnp.int32, (n_slab * CAP, 128), 0)
    placer = jnp.where(spots == target, 1.0, 0.0)
    outgoing[...] = dot_nt(placer, traces[...].reshape(STEPS * PROBES, 128)).reshape(
        n_slab, CAP, STEPS * PROBES
    )

    def to_owner(k):
        other = lax.rem(s + k, n_slab)
        return pltpu.make_async_remote_copy(
            src_ref=outgoing.at[other],
            dst_ref=incoming.at[s],
            send_sem=a2a_send.at[k],
            recv_sem=a2a_recv.at[k],
            device_id={"slab": other},
            device_id_type=MESH,
        )

    to_self = pltpu.make_async_copy(outgoing.at[s], incoming.at[s], own_sem)
    to_self.start()

    @pl.loop(1, n_slab)
    def _(k):
        to_owner(k).start()

    total = finish(sum_a, n_y, copies)
    copies = begin(
        sum_b, n_x, place_x, n_y, lambda other: {"slab": other * n_y + place_y}, total
    )
    total = finish(sum_b, n_x, copies)
    copies = begin(sum_c, n_grp, g, n_y + n_x, lambda other: {"grp": other}, total)
    total = finish(sum_c, n_grp, copies)

    low = lax.broadcasted_iota(jnp.int32, (32, 128), 1) < PROBES
    unit = lax.broadcasted_iota(jnp.int32, (PROBES, 128), 0)
    unit_lane = lax.broadcasted_iota(jnp.int32, (PROBES, 128), 1)
    left = jnp.concatenate([total, pltpu.roll(total, PROBES, 1)], axis=0)
    work = jnp.where(
        unit_lane < PROBES, left, jnp.where(unit_lane - PROBES == unit, 1.0, 0.0)
    )
    parts = [work[8 * b : 8 * b + 8] for b in range(8)]
    sub = lax.broadcasted_iota(jnp.int32, (8, 128), 0)
    for k in range(PROBES):
        b0 = k // 8
        pivot_row = parts[b0][k % 8 : k % 8 + 1, :]
        scaled = pivot_row / pivot_row[:, k : k + 1]
        for b in range(b0, 8):
            factor = parts[b][:, k : k + 1]
            if b == b0:
                factor = jnp.where(sub > k % 8, factor, 0.0)
            parts[b] = parts[b] - factor * scaled
    work = jnp.concatenate(parts, axis=0)
    diag = jnp.sum(jnp.where(unit == unit_lane, work, 0.0), axis=1, keepdims=True)
    work = work * (1.0 / jnp.sqrt(diag))
    rows = n_slab * n_grp * recs * STEPS
    upper = jnp.where((unit_lane >= unit) & (unit_lane < PROBES), work, 0.0)
    r_out[...] = upper[:, :PROBES] * (1.0 / math.sqrt(rows))
    inverse = jnp.where(unit_lane >= PROBES, work, 0.0) * math.sqrt(rows)
    pair = jnp.concatenate([pltpu.roll(inverse, PROBES, 1), inverse], axis=0)

    to_self.wait()

    @pl.loop(1, n_slab)
    def _(k):
        to_owner(k).wait()

    for half in range(2):
        block = incoming[:, :, pl.ds(128 * half, 128)].reshape(n_slab * CAP, 128)
        q_out[:, pl.ds(128 * half, 128)] = dot_nt(block, pair)

    for c in range(CHUNKS):
        pltpu.make_async_copy(
            stage.at[c], wave_out.at[pl.ds(c * CHUNK, CHUNK)], store_sem.at[c]
        ).wait()


def solution(mesh):
    n_grp = mesh.shape["grp"]
    n_slab = mesh.shape["slab"]

    def per_device(probes, courant, rec_cell, rec_owner, trace_weight):
        recs = rec_cell.shape[0]
        f32 = jnp.float32
        weight = jnp.pad(trace_weight, (0, 128 - recs)).reshape(1, 128)
        vmem = pl.BlockSpec(memory_space=pltpu.VMEM)
        wave, q_basis, r_factor = pl.pallas_call(
            functools.partial(kernel, n_grp, n_slab),
            out_shape=(
                jax.ShapeDtypeStruct((PROBES, CX * CY, CZ), f32),
                jax.ShapeDtypeStruct((n_slab * CAP, STEPS * PROBES), f32),
                jax.ShapeDtypeStruct((PROBES, PROBES), f32),
            ),
            in_specs=[
                pl.BlockSpec(memory_space=pl.ANY),
                vmem,
                pl.BlockSpec(memory_space=pltpu.SMEM),
                vmem,
                vmem,
            ],
            out_specs=(pl.BlockSpec(memory_space=pl.ANY), vmem, vmem),
            scratch_shapes=[
                pltpu.VMEM((CHUNKS, CHUNK, CX * CY, CZ), f32),
                pltpu.VMEM((2, CHUNKS, CHUNK, WIDTH * CY, CZ), f32),
                pltpu.VMEM((STEPS + 1, CHUNKS, CX + 2 * WIDTH, CY, CHUNK, CZ), f32),
                pltpu.VMEM((CX * CY, CHUNK, CZ), f32),
                pltpu.VMEM((CX, CY, 8, CZ), f32),
                pltpu.VMEM((STEPS, CHUNKS, 8, 8, 128), f32),
                pltpu.VMEM((2, STEPS, CHUNKS, 8, 8, 128), f32),
                pltpu.VMEM((8, 8, 128), f32),
                pltpu.VMEM((128, 128), f32),
                pltpu.VMEM((STEPS, PROBES, 128), f32),
                pltpu.VMEM((n_slab, CAP, STEPS * PROBES), f32),
                pltpu.VMEM((n_slab, CAP, STEPS * PROBES), f32),
                pltpu.VMEM((8, 32, 128), f32),
                pltpu.VMEM((n_slab // 8, 32, 128), f32),
                pltpu.VMEM((n_grp, 32, 128), f32),
                pltpu.SemaphoreType.DMA((CHUNKS,)),
                pltpu.SemaphoreType.DMA((CHUNKS,)),
                pltpu.SemaphoreType.DMA((2, CHUNKS)),
                pltpu.SemaphoreType.DMA((2, STEPS, CHUNKS)),
                pltpu.SemaphoreType.DMA((2, CHUNKS)),
                pltpu.SemaphoreType.DMA((2, STEPS, CHUNKS)),
                pltpu.SemaphoreType.DMA((n_slab,)),
                pltpu.SemaphoreType.DMA((n_slab,)),
                pltpu.SemaphoreType.DMA,
                pltpu.SemaphoreType.DMA((8 + n_slab // 8 + n_grp,)),
                pltpu.SemaphoreType.DMA((8 + n_slab // 8 + n_grp,)),
            ],
            compiler_params=pltpu.CompilerParams(
                collective_id=0, has_side_effects=True, vmem_limit_bytes=56 * 1024 * 1024
            ),
        )(
            probes.reshape(PROBES, CX * CY, CZ),
            courant,
            rec_cell,
            rec_owner,
            weight,
        )
        return (wave.reshape(PROBES, CX, CY, CZ), q_basis, r_factor)

    return jax.shard_map(
        per_device,
        mesh=mesh,
        in_specs=(
            P(None, "slab", None, "grp"),
            P("slab", None, "grp"),
            P(("grp", "slab")),
            P(("grp", "slab"), None),
            P(("grp", "slab")),
        ),
        out_specs=(P(None, "slab", None, "grp"), P(("grp", "slab"), None), P()),
        check_vma=False,
    )
```

```python
import functools
import math

import jax
import jax.numpy as jnp
from jax import lax
from jax.experimental import pallas as pl
from jax.experimental.pallas import tpu as pltpu
from jax.sharding import PartitionSpec as P
import numpy as np
import ml_dtypes

PROBES = 64
CX = 16
CY = 8
CZ = 128
STEPS = 4
CHUNK = 8
CHUNKS = PROBES // CHUNK
GROUP = 4
WIDTH = 4
CAP = 8
MESH = pl.DeviceIdType.MESH
EXACT = lax.Precision.HIGHEST

A0 = -205.0 / 72.0
A = (0.0, 8.0 / 5.0, -1.0 / 5.0, 8.0 / 315.0, -1.0 / 560.0)


def halves(value):
    high = float(np.float32(value).astype(ml_dtypes.bfloat16))
    low = float(np.float32(value - high).astype(ml_dtypes.bfloat16))
    return high, low


def banded(gap, low_part, coefficients):
    table = jnp.zeros(gap.shape, jnp.float32)
    for k, value in enumerate(coefficients):
        high, low = halves(value)
        table = jnp.where(gap == k, jnp.where(low_part, low, high), table)
    return table


def split(value):
    high = value.astype(jnp.bfloat16)
    low = (value - high.astype(jnp.float32)).astype(jnp.bfloat16)
    return high, low


def dot_nt(a, b):
    return lax.dot_general(
        a, b, (((1,), (1,)), ((), ())), precision=EXACT, preferred_element_type=jnp.float32
    )


def kernel(
    n_grp,
    n_slab,
    probes,
    courant,
    cell,
    owner,
    weight,
    wave_out,
    q_out,
    r_out,
    field,
    parts_of,
    z_band,
    row_of,
    turn_of,
    latest,
    speed,
    z_own,
    z_halo,
    z_fix,
    z_map,
    traces,
    outgoing,
    incoming,
    sum_a,
    sum_b,
    sum_c,
    load_sem,
    store_sem,
    x_send,
    x_recv,
    z_send,
    z_recv,
    a2a_send,
    a2a_recv,
    own_sem,
    sum_send,
    sum_recv,
):
    s = lax.axis_index("slab")
    g = lax.axis_index("grp")
    has = ((s > 0, s < n_slab - 1), (g > 0, g < n_grp - 1))

    def load(c, p):
        return pltpu.make_async_copy(
            probes.at[c * CHUNK + p], field.at[0, c, pl.ds(WIDTH, CX), :, p], load_sem.at[c]
        )

    def loaded(c):
        whole = field.at[0, c, pl.ds(WIDTH, CX)]
        return pltpu.make_async_copy(whole, whole, load_sem.at[c])

    for c in range(CHUNKS):
        for p in range(CHUNK):
            load(c, p).start()

    barrier = pltpu.get_barrier_semaphore()

    @pl.loop(1, n_slab)
    def _(k):
        pl.semaphore_signal(
            barrier, inc=1, device_id={"slab": lax.rem(s + k, n_slab)}, device_id_type=MESH
        )

    @pl.loop(1, n_grp)
    def _(k):
        pl.semaphore_signal(
            barrier, inc=1, device_id={"grp": lax.rem(g + k, n_grp)}, device_id_type=MESH
        )

    lane = lax.broadcasted_iota(jnp.int32, (8, 128), 1)
    edge = (lane < WIDTH) | (lane >= CZ - WIDTH)
    lane_slot = lane // 8
    low_half = (lane % 8) < WIDTH

    row_i = lax.broadcasted_iota(jnp.int32, (256, 256), 0) % 128
    col_i = lax.broadcasted_iota(jnp.int32, (256, 256), 1)
    low_part = col_i >= 128
    col_i = col_i % 128
    gap = jnp.abs(row_i - col_i)
    crossing = (row_i // 8 == col_i // 8) & ((row_i % 8 < WIDTH) != (col_i % 8 < WIDTH))
    z_band[...] = banded(gap, low_part, (3.0 * A0,) + A[1:]).astype(jnp.bfloat16)
    z_map[...] = jnp.where(crossing, banded(gap, low_part, A), 0.0).astype(jnp.bfloat16)

    recs = cell.shape[0]

    @pl.loop(0, recs)
    def _(r):
        where = cell[r]
        row_of[r] = where // CZ
        turn_of[r] = (r + CZ - where % CZ) % CZ

    latest[...] = jnp.zeros(latest.shape, jnp.float32)

    @pl.loop(0, CX)
    def _(x):
        for y in range(CY):
            speed[x, y] = jnp.broadcast_to(courant[x, pl.ds(y, 1), :], (8, 128))

    blank = jnp.zeros((WIDTH, CY, 8, 128), jnp.float32)
    for side in range(2):

        @pl.when(jnp.logical_not(has[0][side]))
        def _(side=side):
            @pl.loop(0, STEPS)
            def _(t):
                @pl.loop(0, CHUNKS)
                def _(c):
                    field[t, c, pl.ds(side * (CX + WIDTH), WIDTH)] = blank

        @pl.when(jnp.logical_not(has[1][side]))
        def _(side=side):
            @pl.loop(0, STEPS)
            def _(t):
                @pl.loop(0, CHUNKS)
                def _(c):
                    z_halo[side, t, c] = jnp.zeros((8, 8, 128), jnp.float32)

    def x_copy(t, c, way):
        return pltpu.make_async_remote_copy(
            src_ref=field.at[t, c, pl.ds(WIDTH + (1 - way) * (CX - WIDTH), WIDTH)],
            dst_ref=field.at[t, c, pl.ds(way * (CX + WIDTH), WIDTH)],
            send_sem=x_send.at[way, c],
            recv_sem=x_recv.at[way, t, c],
            device_id={"slab": s + 1 - 2 * way},
            device_id_type=MESH,
        )

    def z_copy(t, c, way):
        return pltpu.make_async_remote_copy(
            src_ref=z_own.at[t, c, pl.ds(1, 8)],
            dst_ref=z_halo.at[way, t, c],
            send_sem=z_send.at[way, c],
            recv_sem=z_recv.at[way, t, c],
            device_id={"grp": g + 1 - 2 * way},
            device_id_type=MESH,
        )

    def sending(axis, way):
        return has[axis][1 - way]

    def receiving(axis, way):
        return has[axis][way]

    pl.semaphore_wait(barrier, n_slab - 1 + n_grp - 1)

    def pack(values):
        packed = jnp.zeros((8, 128), jnp.float32)
        for i, value in enumerate(values):
            packed = jnp.where(
                lane_slot == i, pltpu.roll(value, (4 + 8 * i) % 128, 1), packed
            )
        return packed

    def keep_parts(c, j, values):
        for i in range(0, 16, 2):
            high, low = split(jnp.concatenate(values[i : i + 2], axis=0))
            spot = pl.ds(pl.multiple_of(128 * j + 8 * i, 16), 16)
            parts_of[c, spot, pl.ds(0, 128)] = high
            parts_of[c, spot, pl.ds(128, 128)] = low

    def bring_in(c):
        loaded(c).wait()
        for way in range(2):

            @pl.when(sending(0, way))
            def _(way=way):
                x_copy(0, c, way).start()

        @pl.loop(0, CX // 2)
        def _(j):
            values = [field[0, c, WIDTH + 2 * j + i // 8, i % 8] for i in range(16)]
            z_own[0, c, j + 1] = pack(values)
            keep_parts(c, j, values)

        for way in range(2):

            @pl.when(sending(1, way))
            def _(way=way):
                z_copy(0, c, way).start()

    @pl.loop(0, GROUP)
    def _(c):
        bring_in(c)

    weights = jnp.zeros((1, 128), jnp.float32)
    for r in range(recs):
        weights = jnp.where(lane[:1] == r, weight[r], weights)

    def store(c, p):
        return pltpu.make_async_copy(
            field.at[STEPS, c, pl.ds(WIDTH, CX), :, p], wave_out.at[c * CHUNK + p], store_sem.at[c]
        )

    def advance(c, t):
        for way in range(2):

            @pl.when(receiving(0, way))
            def _(way=way):
                x_copy(t, c, way).wait_recv()

            @pl.when(receiving(1, way))
            def _(way=way):
                z_copy(t, c, way).wait_recv()

        left = z_halo[0, t, c].reshape(64, 128)
        right = z_halo[1, t, c].reshape(64, 128)
        half = lax.broadcasted_iota(jnp.int32, (64, 128), 1) % 8 < WIDTH
        high, low = split(jnp.where(half, left, right))
        both = jnp.dot(
            jnp.concatenate([high, low], axis=1), z_map[...], preferred_element_type=jnp.float32
        )
        z_fix[...] = (both[:, :128] + both[:, 128:]).reshape(8, 8, 128)
        before = jnp.maximum(t - 1, 0)

        @pl.loop(0, CX // 2)
        def _(j):
            fix = z_fix[j]
            earlier = pl.multiple_of(16 * jnp.maximum(j - 1, 0), 16)

            @pl.when(t < STEPS - 1)
            def _():
                z_own[t + 1, c, j] = pack([latest[earlier + i] for i in range(16)])

            rows = parts_of[c, pl.ds(pl.multiple_of(128 * j, 128), 128), :]
            both = jnp.dot(rows, z_band[...], preferred_element_type=jnp.float32)
            along_z = both[:, :128] + both[:, 128:]
            values = []
            for i in range(16):
                y = i % 8
                x = 2 * j + i // 8

                def at(dx, dy):
                    return field[t, c, WIDTH + x + dx, y + dy]

                center = at(0, 0)
                total = along_z[8 * i : 8 * i + 8]
                for k in range(1, 5):
                    beside = at(k, 0) + at(-k, 0)
                    if y + k < CY:
                        beside = beside + at(0, k)
                    if y - k >= 0:
                        beside = beside + at(0, -k)
                    total = total + A[k] * beside
                correction = pltpu.roll(fix, (128 - 4 - 8 * i) % 128, 1)
                total = total + jnp.where(edge, correction, 0.0)
                old = field[before, c, WIDTH + x, y]
                value = (2.0 * center - old) + speed[x, y] * total
                field[t + 1, c, WIDTH + x, y] = value
                latest[16 * j + i] = value
                values.append(value)

            keep_parts(c, j, values)

        @pl.when(t < STEPS - 1)
        def _():
            z_own[t + 1, c, 8] = pack([latest[112 + i] for i in range(16)])
            for way in range(2):

                @pl.when(sending(0, way))
                def _(way=way):
                    x_copy(t, c, way).wait_send()
                    x_copy(t + 1, c, way).start()

                @pl.when(sending(1, way))
                def _(way=way):
                    z_copy(t, c, way).wait_send()
                    z_copy(t + 1, c, way).start()

        @pl.when(t == STEPS - 1)
        def _():
            for way in range(2):

                @pl.when(sending(0, way))
                def _(way=way):
                    x_copy(t, c, way).wait_send()

                @pl.when(sending(1, way))
                def _(way=way):
                    z_copy(t, c, way).wait_send()

        found = jnp.zeros((8, 128), jnp.float32)
        for r in range(recs):
            value = pltpu.roll(latest[row_of[r]], turn_of[r], 1)
            found = jnp.where(lane == r, value, found)
        traces[t, pl.ds(c * CHUNK, CHUNK), :] = found * weights

        @pl.when(t == STEPS - 1)
        def _():
            for p in range(CHUNK):
                store(c, p).start()

    @pl.loop(0, CHUNKS * STEPS)
    def _(n):
        block = n // (GROUP * STEPS)
        t = n % (GROUP * STEPS) // GROUP
        c = block * GROUP + n % GROUP
        advance(c, t)

        @pl.when((t == STEPS - 1) & (block < CHUNKS // GROUP - 1))
        def _():
            bring_in(c + GROUP)

    gram = jnp.zeros((PROBES, PROBES), jnp.float32)
    for t in range(STEPS):
        gram = gram + dot_nt(traces[t], traces[t])
    folded = jnp.concatenate([gram[:32], gram[32:]], axis=1)

    n_y = 8
    place_y = s % n_y
    place_x = s // n_y

    def stage_copies(buffer, count, me, base, device):
        def one(k):
            return pltpu.make_async_remote_copy(
                src_ref=buffer.at[me],
                dst_ref=buffer.at[me],
                send_sem=sum_send.at[base + k],
                recv_sem=sum_recv.at[base + k],
                device_id=device(lax.rem(me + k, count)),
                device_id_type=MESH,
            )

        return [one(k) for k in range(1, count)]

    def begin(buffer, count, me, base, device, value):
        buffer[me] = value
        copies = stage_copies(buffer, count, me, base, device)
        for copy in copies:
            copy.start()
        return copies

    def finish(buffer, count, copies):
        for copy in copies:
            copy.wait_recv()
        total = buffer[0]
        for k in range(1, count):
            total = total + buffer[k]
        for copy in copies:
            copy.wait_send()
        return total

    n_x = n_slab // n_y
    copies = begin(
        sum_a, n_y, place_y, 0, lambda other: {"slab": place_x * n_y + other}, folded
    )

    own_row = jnp.zeros((1, 128), jnp.int32)
    for r in range(recs):
        own_row = jnp.where(lane[:1] == r, owner[r], own_row)
    slot = jnp.zeros((1, 128), jnp.int32)
    for r in range(recs):
        slot = slot + jnp.where((own_row == owner[r]) & (lane[:1] > r), 1, 0)
    lane_row = lax.broadcasted_iota(jnp.int32, (1, 128), 1)
    target = jnp.where(lane_row < recs, own_row * CAP + slot, -1)
    spots = lax.broadcasted_iota(jnp.int32, (n_slab * CAP, 128), 0)
    placer = jnp.where(spots == target, 1.0, 0.0)
    outgoing[...] = dot_nt(placer, traces[...].reshape(STEPS * PROBES, 128)).reshape(
        n_slab, CAP, STEPS * PROBES
    )

    def to_owner(k):
        other = lax.rem(s + k, n_slab)
        return pltpu.make_async_remote_copy(
            src_ref=outgoing.at[other],
            dst_ref=incoming.at[s],
            send_sem=a2a_send.at[k],
            recv_sem=a2a_recv.at[k],
            device_id={"slab": other},
            device_id_type=MESH,
        )

    to_self = pltpu.make_async_copy(outgoing.at[s], incoming.at[s], own_sem)
    to_self.start()

    @pl.loop(1, n_slab)
    def _(k):
        to_owner(k).start()

    total = finish(sum_a, n_y, copies)
    copies = begin(
        sum_b, n_x, place_x, n_y, lambda other: {"slab": other * n_y + place_y}, total
    )
    total = finish(sum_b, n_x, copies)
    copies = begin(sum_c, n_grp, g, n_y + n_x, lambda other: {"grp": other}, total)
    total = finish(sum_c, n_grp, copies)

    low = lax.broadcasted_iota(jnp.int32, (32, 128), 1) < PROBES
    unit = lax.broadcasted_iota(jnp.int32, (PROBES, 128), 0)
    unit_lane = lax.broadcasted_iota(jnp.int32, (PROBES, 128), 1)
    left = jnp.concatenate([total, pltpu.roll(total, PROBES, 1)], axis=0)
    work = jnp.where(
        unit_lane < PROBES, left, jnp.where(unit_lane - PROBES == unit, 1.0, 0.0)
    )
    parts = [work[8 * b : 8 * b + 8] for b in range(8)]
    sub = lax.broadcasted_iota(jnp.int32, (8, 128), 0)
    for k in range(PROBES):
        b0 = k // 8
        pivot_row = parts[b0][k % 8 : k % 8 + 1, :]
        scaled = pivot_row / pivot_row[:, k : k + 1]
        for b in range(b0, 8):
            factor = parts[b][:, k : k + 1]
            if b == b0:
                factor = jnp.where(sub > k % 8, factor, 0.0)
            parts[b] = parts[b] - factor * scaled
    work = jnp.concatenate(parts, axis=0)
    diag = jnp.sum(jnp.where(unit == unit_lane, work, 0.0), axis=1, keepdims=True)
    work = work * (1.0 / jnp.sqrt(diag))
    rows = n_slab * n_grp * recs * STEPS
    upper = jnp.where((unit_lane >= unit) & (unit_lane < PROBES), work, 0.0)
    r_out[...] = upper[:, :PROBES] * (1.0 / math.sqrt(rows))
    inverse = jnp.where(unit_lane >= PROBES, work, 0.0) * math.sqrt(rows)
    pair = jnp.concatenate([pltpu.roll(inverse, PROBES, 1), inverse], axis=0)

    to_self.wait()

    @pl.loop(1, n_slab)
    def _(k):
        to_owner(k).wait()

    for half in range(2):
        block = incoming[:, :, pl.ds(128 * half, 128)].reshape(n_slab * CAP, 128)
        q_out[:, pl.ds(128 * half, 128)] = dot_nt(block, pair)

    for c in range(CHUNKS):
        whole = field.at[STEPS, c, pl.ds(WIDTH, CX)]
        pltpu.make_async_copy(whole, whole, store_sem.at[c]).wait()


def solution(mesh):
    n_grp = mesh.shape["grp"]
    n_slab = mesh.shape["slab"]

    def per_device(probes, courant, rec_cell, rec_owner, trace_weight):
        recs = rec_cell.shape[0]
        f32 = jnp.float32
        smem = pl.BlockSpec(memory_space=pltpu.SMEM)
        vmem = pl.BlockSpec(memory_space=pltpu.VMEM)
        wave, q_basis, r_factor = pl.pallas_call(
            functools.partial(kernel, n_grp, n_slab),
            out_shape=(
                jax.ShapeDtypeStruct((PROBES, CX, CY, CZ), f32),
                jax.ShapeDtypeStruct((n_slab * CAP, STEPS * PROBES), f32),
                jax.ShapeDtypeStruct((PROBES, PROBES), f32),
            ),
            in_specs=[
                pl.BlockSpec(memory_space=pl.ANY),
                vmem,
                smem,
                smem,
                smem,
            ],
            out_specs=(pl.BlockSpec(memory_space=pl.ANY), vmem, vmem),
            scratch_shapes=[
                pltpu.VMEM((STEPS + 1, CHUNKS, CX + 2 * WIDTH, CY, CHUNK, CZ), f32),
                pltpu.VMEM((CHUNKS, CX * CY * CHUNK, 2 * CZ), jnp.bfloat16),
                pltpu.VMEM((2 * CZ, 2 * CZ), jnp.bfloat16),
                pltpu.SMEM((recs,), jnp.int32),
                pltpu.SMEM((recs,), jnp.int32),
                pltpu.VMEM((CX * CY, CHUNK, CZ), f32),
                pltpu.VMEM((CX, CY, 8, CZ), f32),
                pltpu.VMEM((STEPS, CHUNKS, 9, 8, 128), f32),
                pltpu.VMEM((2, STEPS, CHUNKS, 8, 8, 128), f32),
                pltpu.VMEM((8, 8, 128), f32),
                pltpu.VMEM((256, 256), jnp.bfloat16),
                pltpu.VMEM((STEPS, PROBES, 128), f32),
                pltpu.VMEM((n_slab, CAP, STEPS * PROBES), f32),
                pltpu.VMEM((n_slab, CAP, STEPS * PROBES), f32),
                pltpu.VMEM((8, 32, 128), f32),
                pltpu.VMEM((n_slab // 8, 32, 128), f32),
                pltpu.VMEM((n_grp, 32, 128), f32),
                pltpu.SemaphoreType.DMA((CHUNKS,)),
                pltpu.SemaphoreType.DMA((CHUNKS,)),
                pltpu.SemaphoreType.DMA((2, CHUNKS)),
                pltpu.SemaphoreType.DMA((2, STEPS, CHUNKS)),
                pltpu.SemaphoreType.DMA((2, CHUNKS)),
                pltpu.SemaphoreType.DMA((2, STEPS, CHUNKS)),
                pltpu.SemaphoreType.DMA((n_slab,)),
                pltpu.SemaphoreType.DMA((n_slab,)),
                pltpu.SemaphoreType.DMA,
                pltpu.SemaphoreType.DMA((8 + n_slab // 8 + n_grp,)),
                pltpu.SemaphoreType.DMA((8 + n_slab // 8 + n_grp,)),
            ],
            compiler_params=pltpu.CompilerParams(
                collective_id=0, has_side_effects=True, vmem_limit_bytes=56 * 1024 * 1024
            ),
        )(
            probes,
            courant,
            rec_cell,
            rec_owner.reshape(recs),
            trace_weight,
        )
        return (wave, q_basis, r_factor)

    return jax.shard_map(
        per_device,
        mesh=mesh,
        in_specs=(
            P(None, "slab", None, "grp"),
            P("slab", None, "grp"),
            P(("grp", "slab")),
            P(("grp", "slab"), None),
            P(("grp", "slab")),
        ),
        out_specs=(P(None, "slab", None, "grp"), P(("grp", "slab"), None), P()),
        check_vma=False,
    )
```

```python
import functools
import math

import jax
import jax.numpy as jnp
from jax import lax
from jax.experimental import pallas as pl
from jax.experimental.pallas import tpu as pltpu
from jax.sharding import PartitionSpec as P
import numpy as np
import ml_dtypes

PROBES = 64
CX = 16
CY = 8
CZ = 128
STEPS = 4
CHUNK = 8
CHUNKS = PROBES // CHUNK
GROUP = 4
WIDTH = 4
CAP = 8
MESH = pl.DeviceIdType.MESH
EXACT = lax.Precision.HIGHEST

A0 = -205.0 / 72.0
A = (0.0, 8.0 / 5.0, -1.0 / 5.0, 8.0 / 315.0, -1.0 / 560.0)


def halves(value):
    high = float(np.float32(value).astype(ml_dtypes.bfloat16))
    low = float(np.float32(value - high).astype(ml_dtypes.bfloat16))
    return high, low


def banded(gap, low_part, coefficients):
    table = jnp.zeros(gap.shape, jnp.float32)
    for k, value in enumerate(coefficients):
        high, low = halves(value)
        table = jnp.where(gap == k, jnp.where(low_part, low, high), table)
    return table


def split(value):
    high = value.astype(jnp.bfloat16)
    low = (value - high.astype(jnp.float32)).astype(jnp.bfloat16)
    return high, low


def dot_nt(a, b):
    return lax.dot_general(
        a, b, (((1,), (1,)), ((), ())), precision=EXACT, preferred_element_type=jnp.float32
    )


def kernel(
    n_grp,
    n_slab,
    probes,
    courant,
    cell,
    owner,
    weight,
    wave_out,
    q_out,
    r_out,
    field_0,
    field_1,
    field_2,
    field_3,
    field_4,
    parts_of,
    z_band,
    z_lap,
    row_of,
    turn_of,
    latest,
    speed,
    z_own,
    z_halo,
    z_fix,
    z_map,
    traces,
    outgoing,
    incoming,
    sum_a,
    sum_b,
    sum_c,
    load_sem,
    store_sem,
    x_send,
    x_recv,
    z_send,
    z_recv,
    a2a_send,
    a2a_recv,
    own_sem,
    sum_send,
    sum_recv,
):
    field = (field_0, field_1, field_2, field_3, field_4)
    s = lax.axis_index("slab")
    g = lax.axis_index("grp")
    has = ((s > 0, s < n_slab - 1), (g > 0, g < n_grp - 1))

    def load(c, p):
        return pltpu.make_async_copy(
            probes.at[c * CHUNK + p], field[0].at[c, pl.ds(WIDTH, CX), :, p], load_sem.at[c]
        )

    def loaded(c):
        whole = field[0].at[c, pl.ds(WIDTH, CX)]
        return pltpu.make_async_copy(whole, whole, load_sem.at[c])

    for c in range(CHUNKS):
        for p in range(CHUNK):
            load(c, p).start()

    barrier = pltpu.get_barrier_semaphore()

    @pl.loop(1, n_slab)
    def _(k):
        pl.semaphore_signal(
            barrier, inc=1, device_id={"slab": lax.rem(s + k, n_slab)}, device_id_type=MESH
        )

    @pl.loop(1, n_grp)
    def _(k):
        pl.semaphore_signal(
            barrier, inc=1, device_id={"grp": lax.rem(g + k, n_grp)}, device_id_type=MESH
        )

    lane = lax.broadcasted_iota(jnp.int32, (8, 128), 1)
    edge = (lane < WIDTH) | (lane >= CZ - WIDTH)
    lane_slot = lane // 8
    low_half = (lane % 8) < WIDTH

    row_i = lax.broadcasted_iota(jnp.int32, (256, 256), 0) % 128
    col_i = lax.broadcasted_iota(jnp.int32, (256, 256), 1)
    low_part = col_i >= 128
    col_i = col_i % 128
    gap = jnp.abs(row_i - col_i)
    crossing = (row_i // 8 == col_i // 8) & ((row_i % 8 < WIDTH) != (col_i % 8 < WIDTH))
    z_band[...] = banded(gap, low_part, (3.0 * A0,) + A[1:]).astype(jnp.bfloat16)
    z_map[...] = jnp.where(crossing, banded(gap, low_part, A), 0.0).astype(jnp.bfloat16)

    recs = cell.shape[0]

    @pl.loop(0, recs)
    def _(r):
        where = cell[r]
        row_of[r] = where // CZ
        turn_of[r] = (r + CZ - where % CZ) % CZ

    latest[...] = jnp.zeros(latest.shape, jnp.float32)

    @pl.loop(0, CX)
    def _(x):
        for y in range(CY):
            speed[x, y] = jnp.broadcast_to(courant[x, pl.ds(y, 1), :], (8, 128))

    blank = jnp.zeros((WIDTH, CY, 8, 128), jnp.float32)
    for side in range(2):

        @pl.when(jnp.logical_not(has[0][side]))
        def _(side=side):
            @pl.loop(0, CHUNKS)
            def _(c):
                for t in range(STEPS):
                    field[t][c, pl.ds(side * (CX + WIDTH), WIDTH)] = blank

        @pl.when(jnp.logical_not(has[1][side]))
        def _(side=side):
            @pl.loop(0, STEPS)
            def _(t):
                @pl.loop(0, CHUNKS)
                def _(c):
                    z_halo[side, t, c] = jnp.zeros((8, 8, 128), jnp.float32)

    def x_copy(t, c, way):
        return pltpu.make_async_remote_copy(
            src_ref=field[t].at[c, pl.ds(WIDTH + (1 - way) * (CX - WIDTH), WIDTH)],
            dst_ref=field[t].at[c, pl.ds(way * (CX + WIDTH), WIDTH)],
            send_sem=x_send.at[way, c],
            recv_sem=x_recv.at[way, t, c],
            device_id={"slab": s + 1 - 2 * way},
            device_id_type=MESH,
        )

    def z_copy(t, c, way):
        return pltpu.make_async_remote_copy(
            src_ref=z_own.at[t, c, pl.ds(1, 8)],
            dst_ref=z_halo.at[way, t, c],
            send_sem=z_send.at[way, c],
            recv_sem=z_recv.at[way, t, c],
            device_id={"grp": g + 1 - 2 * way},
            device_id_type=MESH,
        )

    def sending(axis, way):
        return has[axis][1 - way]

    def receiving(axis, way):
        return has[axis][way]

    pl.semaphore_wait(barrier, n_slab - 1 + n_grp - 1)

    def pack(values):
        packed = jnp.zeros((8, 128), jnp.float32)
        for i, value in enumerate(values):
            packed = jnp.where(
                lane_slot == i, pltpu.roll(value, (4 + 8 * i) % 128, 1), packed
            )
        return packed

    def keep_parts(c, j, values):
        for i in range(0, 16, 2):
            high, low = split(jnp.concatenate(values[i : i + 2], axis=0))
            spot = pl.ds(pl.multiple_of(128 * j + 8 * i, 16), 16)
            parts_of[c, spot, pl.ds(0, 128)] = high
            parts_of[c, spot, pl.ds(128, 128)] = low

    def bring_in(c):
        loaded(c).wait()
        for way in range(2):

            @pl.when(sending(0, way))
            def _(way=way):
                x_copy(0, c, way).start()

        @pl.loop(0, CX // 2)
        def _(j):
            values = [field[0][c, WIDTH + 2 * j + i // 8, i % 8] for i in range(16)]
            z_own[0, c, j + 1] = pack(values)
            keep_parts(c, j, values)

        for way in range(2):

            @pl.when(sending(1, way))
            def _(way=way):
                z_copy(0, c, way).start()

    @pl.loop(0, GROUP)
    def _(c):
        bring_in(c)

    weights = jnp.zeros((1, 128), jnp.float32)
    for r in range(recs):
        weights = jnp.where(lane[:1] == r, weight[r], weights)

    def store(c, p):
        return pltpu.make_async_copy(
            field[STEPS].at[c, pl.ds(WIDTH, CX), :, p], wave_out.at[c * CHUNK + p], store_sem.at[c]
        )

    def advance(c, t):
        for way in range(2):

            @pl.when(receiving(0, way))
            def _(way=way):
                x_copy(t, c, way).wait_recv()

            @pl.when(receiving(1, way))
            def _(way=way):
                z_copy(t, c, way).wait_recv()

        left = z_halo[0, t, c].reshape(64, 128)
        right = z_halo[1, t, c].reshape(64, 128)
        half = lax.broadcasted_iota(jnp.int32, (64, 128), 1) % 8 < WIDTH
        high, low = split(jnp.where(half, left, right))
        both = jnp.dot(
            jnp.concatenate([high, low], axis=1), z_map[...], preferred_element_type=jnp.float32
        )
        z_fix[...] = (both[:, :128] + both[:, 128:]).reshape(8, 8, 128)
        before = max(t - 1, 0)
        both = jnp.dot(parts_of[c], z_band[...], preferred_element_type=jnp.float32)
        z_lap[...] = both[:, :128] + both[:, 128:]

        @pl.loop(0, CX // 2)
        def _(j):
            fix = z_fix[j]
            earlier = pl.multiple_of(16 * jnp.maximum(j - 1, 0), 16)

            if t < STEPS - 1:
                z_own[t + 1, c, j] = pack([latest[earlier + i] for i in range(16)])

            along_z = z_lap[pl.ds(pl.multiple_of(128 * j, 128), 128), :]
            values = []
            for i in range(16):
                y = i % 8
                x = 2 * j + i // 8

                def at(dx, dy):
                    return field[t][c, WIDTH + x + dx, y + dy]

                center = at(0, 0)
                total = along_z[8 * i : 8 * i + 8]
                for k in range(1, 5):
                    beside = at(k, 0) + at(-k, 0)
                    if y + k < CY:
                        beside = beside + at(0, k)
                    if y - k >= 0:
                        beside = beside + at(0, -k)
                    total = total + A[k] * beside
                correction = pltpu.roll(fix, (128 - 4 - 8 * i) % 128, 1)
                total = total + jnp.where(edge, correction, 0.0)
                old = field[before][c, WIDTH + x, y]
                value = (2.0 * center - old) + speed[x, y] * total
                field[t + 1][c, WIDTH + x, y] = value
                latest[16 * j + i] = value
                values.append(value)

            if t < STEPS - 1:
                keep_parts(c, j, values)

        if t < STEPS - 1:
            z_own[t + 1, c, 8] = pack([latest[112 + i] for i in range(16)])
            for way in range(2):

                @pl.when(sending(0, way))
                def _(way=way):
                    x_copy(t, c, way).wait_send()
                    x_copy(t + 1, c, way).start()

                @pl.when(sending(1, way))
                def _(way=way):
                    z_copy(t, c, way).wait_send()
                    z_copy(t + 1, c, way).start()

        if t == STEPS - 1:
            for way in range(2):

                @pl.when(sending(0, way))
                def _(way=way):
                    x_copy(t, c, way).wait_send()

                @pl.when(sending(1, way))
                def _(way=way):
                    z_copy(t, c, way).wait_send()

        found = jnp.zeros((8, 128), jnp.float32)
        for r in range(recs):
            value = pltpu.roll(latest[row_of[r]], turn_of[r], 1)
            found = jnp.where(lane == r, value, found)
        traces[t, pl.ds(c * CHUNK, CHUNK), :] = found * weights

        if t == STEPS - 1:
            for p in range(CHUNK):
                store(c, p).start()

    @pl.loop(0, CHUNKS // GROUP)
    def _(block):
        for t in range(STEPS):

            @pl.loop(0, GROUP)
            def _(k, t=t):
                c = block * GROUP + k
                advance(c, t)
                if t == STEPS - 1:

                    @pl.when(block < CHUNKS // GROUP - 1)
                    def _():
                        bring_in(c + GROUP)

    gram = jnp.zeros((PROBES, PROBES), jnp.float32)
    for t in range(STEPS):
        gram = gram + dot_nt(traces[t], traces[t])
    folded = jnp.concatenate([gram[:32], gram[32:]], axis=1)

    n_y = 8
    place_y = s % n_y
    place_x = s // n_y

    def stage_copies(buffer, count, me, base, device):
        def one(k):
            return pltpu.make_async_remote_copy(
                src_ref=buffer.at[me],
                dst_ref=buffer.at[me],
                send_sem=sum_send.at[base + k],
                recv_sem=sum_recv.at[base + k],
                device_id=device(lax.rem(me + k, count)),
                device_id_type=MESH,
            )

        return [one(k) for k in range(1, count)]

    def begin(buffer, count, me, base, device, value):
        buffer[me] = value
        copies = stage_copies(buffer, count, me, base, device)
        for copy in copies:
            copy.start()
        return copies

    def finish(buffer, count, copies):
        for copy in copies:
            copy.wait_recv()
        total = buffer[0]
        for k in range(1, count):
            total = total + buffer[k]
        for copy in copies:
            copy.wait_send()
        return total

    n_x = n_slab // n_y
    copies = begin(
        sum_a, n_y, place_y, 0, lambda other: {"slab": place_x * n_y + other}, folded
    )

    own_row = jnp.zeros((1, 128), jnp.int32)
    for r in range(recs):
        own_row = jnp.where(lane[:1] == r, owner[r], own_row)
    slot = jnp.zeros((1, 128), jnp.int32)
    for r in range(recs):
        slot = slot + jnp.where((own_row == owner[r]) & (lane[:1] > r), 1, 0)
    lane_row = lax.broadcasted_iota(jnp.int32, (1, 128), 1)
    target = jnp.where(lane_row < recs, own_row * CAP + slot, -1)
    spots = lax.broadcasted_iota(jnp.int32, (n_slab * CAP, 128), 0)
    placer = jnp.where(spots == target, 1.0, 0.0)
    outgoing[...] = dot_nt(placer, traces[...].reshape(STEPS * PROBES, 128)).reshape(
        n_slab, CAP, STEPS * PROBES
    )

    def to_owner(k):
        other = lax.rem(s + k, n_slab)
        return pltpu.make_async_remote_copy(
            src_ref=outgoing.at[other],
            dst_ref=incoming.at[s],
            send_sem=a2a_send.at[k],
            recv_sem=a2a_recv.at[k],
            device_id={"slab": other},
            device_id_type=MESH,
        )

    to_self = pltpu.make_async_copy(outgoing.at[s], incoming.at[s], own_sem)
    to_self.start()

    @pl.loop(1, n_slab)
    def _(k):
        to_owner(k).start()

    total = finish(sum_a, n_y, copies)
    copies = begin(
        sum_b, n_x, place_x, n_y, lambda other: {"slab": other * n_y + place_y}, total
    )
    total = finish(sum_b, n_x, copies)
    copies = begin(sum_c, n_grp, g, n_y + n_x, lambda other: {"grp": other}, total)
    total = finish(sum_c, n_grp, copies)

    low = lax.broadcasted_iota(jnp.int32, (32, 128), 1) < PROBES
    unit = lax.broadcasted_iota(jnp.int32, (PROBES, 128), 0)
    unit_lane = lax.broadcasted_iota(jnp.int32, (PROBES, 128), 1)
    left = jnp.concatenate([total, pltpu.roll(total, PROBES, 1)], axis=0)
    work = jnp.where(
        unit_lane < PROBES, left, jnp.where(unit_lane - PROBES == unit, 1.0, 0.0)
    )
    parts = [work[8 * b : 8 * b + 8] for b in range(8)]
    sub = lax.broadcasted_iota(jnp.int32, (8, 128), 0)
    for k in range(PROBES):
        b0 = k // 8
        pivot_row = parts[b0][k % 8 : k % 8 + 1, :]
        scaled = pivot_row / pivot_row[:, k : k + 1]
        for b in range(b0, 8):
            factor = parts[b][:, k : k + 1]
            if b == b0:
                factor = jnp.where(sub > k % 8, factor, 0.0)
            parts[b] = parts[b] - factor * scaled
    work = jnp.concatenate(parts, axis=0)
    diag = jnp.sum(jnp.where(unit == unit_lane, work, 0.0), axis=1, keepdims=True)
    work = work * (1.0 / jnp.sqrt(diag))
    rows = n_slab * n_grp * recs * STEPS
    upper = jnp.where((unit_lane >= unit) & (unit_lane < PROBES), work, 0.0)
    r_out[...] = upper[:, :PROBES] * (1.0 / math.sqrt(rows))
    inverse = jnp.where(unit_lane >= PROBES, work, 0.0) * math.sqrt(rows)
    pair = jnp.concatenate([pltpu.roll(inverse, PROBES, 1), inverse], axis=0)

    to_self.wait()

    @pl.loop(1, n_slab)
    def _(k):
        to_owner(k).wait()

    for half in range(2):
        block = incoming[:, :, pl.ds(128 * half, 128)].reshape(n_slab * CAP, 128)
        q_out[:, pl.ds(128 * half, 128)] = dot_nt(block, pair)

    for c in range(CHUNKS):
        whole = field[STEPS].at[c, pl.ds(WIDTH, CX)]
        pltpu.make_async_copy(whole, whole, store_sem.at[c]).wait()


def solution(mesh):
    n_grp = mesh.shape["grp"]
    n_slab = mesh.shape["slab"]

    def per_device(probes, courant, rec_cell, rec_owner, trace_weight):
        recs = rec_cell.shape[0]
        f32 = jnp.float32
        smem = pl.BlockSpec(memory_space=pltpu.SMEM)
        vmem = pl.BlockSpec(memory_space=pltpu.VMEM)
        wave, q_basis, r_factor = pl.pallas_call(
            functools.partial(kernel, n_grp, n_slab),
            out_shape=(
                jax.ShapeDtypeStruct((PROBES, CX, CY, CZ), f32),
                jax.ShapeDtypeStruct((n_slab * CAP, STEPS * PROBES), f32),
                jax.ShapeDtypeStruct((PROBES, PROBES), f32),
            ),
            in_specs=[
                pl.BlockSpec(memory_space=pl.ANY),
                vmem,
                smem,
                smem,
                smem,
            ],
            out_specs=(pl.BlockSpec(memory_space=pl.ANY), vmem, vmem),
            scratch_shapes=[pltpu.VMEM((CHUNKS, CX + 2 * WIDTH, CY, CHUNK, CZ), f32)] * (STEPS + 1)
            + [
                pltpu.VMEM((CHUNKS, CX * CY * CHUNK, 2 * CZ), jnp.bfloat16),
                pltpu.VMEM((2 * CZ, 2 * CZ), jnp.bfloat16),
                pltpu.VMEM((CX * CY * CHUNK, CZ), f32),
                pltpu.SMEM((recs,), jnp.int32),
                pltpu.SMEM((recs,), jnp.int32),
                pltpu.VMEM((CX * CY, CHUNK, CZ), f32),
                pltpu.VMEM((CX, CY, 8, CZ), f32),
                pltpu.VMEM((STEPS, CHUNKS, 9, 8, 128), f32),
                pltpu.VMEM((2, STEPS, CHUNKS, 8, 8, 128), f32),
                pltpu.VMEM((8, 8, 128), f32),
                pltpu.VMEM((256, 256), jnp.bfloat16),
                pltpu.VMEM((STEPS, PROBES, 128), f32),
                pltpu.VMEM((n_slab, CAP, STEPS * PROBES), f32),
                pltpu.VMEM((n_slab, CAP, STEPS * PROBES), f32),
                pltpu.VMEM((8, 32, 128), f32),
                pltpu.VMEM((n_slab // 8, 32, 128), f32),
                pltpu.VMEM((n_grp, 32, 128), f32),
                pltpu.SemaphoreType.DMA((CHUNKS,)),
                pltpu.SemaphoreType.DMA((CHUNKS,)),
                pltpu.SemaphoreType.DMA((2, CHUNKS)),
                pltpu.SemaphoreType.DMA((2, STEPS, CHUNKS)),
                pltpu.SemaphoreType.DMA((2, CHUNKS)),
                pltpu.SemaphoreType.DMA((2, STEPS, CHUNKS)),
                pltpu.SemaphoreType.DMA((n_slab,)),
                pltpu.SemaphoreType.DMA((n_slab,)),
                pltpu.SemaphoreType.DMA,
                pltpu.SemaphoreType.DMA((8 + n_slab // 8 + n_grp,)),
                pltpu.SemaphoreType.DMA((8 + n_slab // 8 + n_grp,)),
            ],
            compiler_params=pltpu.CompilerParams(
                collective_id=0, has_side_effects=True, vmem_limit_bytes=56 * 1024 * 1024
            ),
        )(
            probes,
            courant,
            rec_cell,
            rec_owner.reshape(recs),
            trace_weight,
        )
        return (wave, q_basis, r_factor)

    return jax.shard_map(
        per_device,
        mesh=mesh,
        in_specs=(
            P(None, "slab", None, "grp"),
            P("slab", None, "grp"),
            P(("grp", "slab")),
            P(("grp", "slab"), None),
            P(("grp", "slab")),
        ),
        out_specs=(P(None, "slab", None, "grp"), P(("grp", "slab"), None), P()),
        check_vma=False,
    )
```

```python
import functools
import math

import jax
import jax.numpy as jnp
from jax import lax
from jax.experimental import pallas as pl
from jax.experimental.pallas import tpu as pltpu
from jax.sharding import PartitionSpec as P
import numpy as np
import ml_dtypes

PROBES = 64
CX = 16
CY = 8
CZ = 128
STEPS = 4
CHUNK = 8
CHUNKS = PROBES // CHUNK
GROUP = 4
WIDTH = 4
CAP = 8
MESH = pl.DeviceIdType.MESH
EXACT = lax.Precision.HIGHEST

A0 = -205.0 / 72.0
A = (0.0, 8.0 / 5.0, -1.0 / 5.0, 8.0 / 315.0, -1.0 / 560.0)


def halves(value):
    high = float(np.float32(value).astype(ml_dtypes.bfloat16))
    low = float(np.float32(value - high).astype(ml_dtypes.bfloat16))
    return high, low


def banded(gap, low_part, coefficients):
    table = jnp.zeros(gap.shape, jnp.float32)
    for k, value in enumerate(coefficients):
        high, low = halves(value)
        table = jnp.where(gap == k, jnp.where(low_part, low, high), table)
    return table


def split(value):
    high = value.astype(jnp.bfloat16)
    low = (value - high.astype(jnp.float32)).astype(jnp.bfloat16)
    return high, low


def dot_nt(a, b):
    return lax.dot_general(
        a, b, (((1,), (1,)), ((), ())), precision=EXACT, preferred_element_type=jnp.float32
    )


def kernel(
    n_grp,
    n_slab,
    probes,
    courant,
    cell,
    owner,
    weight,
    wave_out,
    incoming,
    gram_out,
    field_0,
    field_1,
    field_2,
    field_3,
    field_4,
    parts_of,
    z_band,
    z_lap,
    row_of,
    turn_of,
    latest,
    speed,
    z_own,
    z_halo,
    z_fix,
    z_map,
    traces,
    outgoing,
    shares,
    sum_a,
    sum_b,
    sum_c,
    load_sem,
    store_sem,
    x_send,
    x_recv,
    z_send,
    z_recv,
    a2a_send,
    a2a_recv,
    own_sem,
    sum_send,
    sum_recv,
):
    field = (field_0, field_1, field_2, field_3, field_4)
    s = lax.axis_index("slab")
    g = lax.axis_index("grp")
    has = ((s > 0, s < n_slab - 1), (g > 0, g < n_grp - 1))

    def load(c, p):
        return pltpu.make_async_copy(
            probes.at[c * CHUNK + p], field[0].at[c, pl.ds(WIDTH, CX), :, p], load_sem.at[c]
        )

    def loaded(c):
        whole = field[0].at[c, pl.ds(WIDTH, CX)]
        return pltpu.make_async_copy(whole, whole, load_sem.at[c])

    for c in range(CHUNKS):
        for p in range(CHUNK):
            load(c, p).start()

    barrier = pltpu.get_barrier_semaphore()

    @pl.loop(1, n_slab)
    def _(k):
        pl.semaphore_signal(
            barrier, inc=1, device_id={"slab": lax.rem(s + k, n_slab)}, device_id_type=MESH
        )

    n_y = 8
    n_x = n_slab // n_y
    place_y = s % n_y
    place_x = s // n_y

    @pl.loop(n_x, n_x * n_grp)
    def _(k):
        pl.semaphore_signal(
            barrier,
            inc=1,
            device_id={
                "slab": lax.rem(place_x + k % n_x, n_x) * n_y + place_y,
                "grp": lax.rem(g + k // n_x, n_grp),
            },
            device_id_type=MESH,
        )

    lane = lax.broadcasted_iota(jnp.int32, (8, 128), 1)
    edge = (lane < WIDTH) | (lane >= CZ - WIDTH)
    lane_slot = lane // 8
    low_half = (lane % 8) < WIDTH

    row_i = lax.broadcasted_iota(jnp.int32, (256, 256), 0) % 128
    col_i = lax.broadcasted_iota(jnp.int32, (256, 256), 1)
    low_part = col_i >= 128
    col_i = col_i % 128
    gap = jnp.abs(row_i - col_i)
    crossing = (row_i // 8 == col_i // 8) & ((row_i % 8 < WIDTH) != (col_i % 8 < WIDTH))
    z_band[...] = banded(gap, low_part, (3.0 * A0,) + A[1:]).astype(jnp.bfloat16)
    z_map[...] = jnp.where(crossing, banded(gap, low_part, A), 0.0).astype(jnp.bfloat16)

    recs = cell.shape[0]

    @pl.loop(0, recs)
    def _(r):
        where = cell[r]
        row_of[r] = where // CZ
        turn_of[r] = (r + CZ - where % CZ) % CZ

    latest[...] = jnp.zeros(latest.shape, jnp.float32)

    @pl.loop(0, CX)
    def _(x):
        for y in range(CY):
            speed[x, y] = jnp.broadcast_to(courant[x, pl.ds(y, 1), :], (8, 128))

    blank = jnp.zeros((WIDTH, CY, 8, 128), jnp.float32)
    for side in range(2):

        @pl.when(jnp.logical_not(has[0][side]))
        def _(side=side):
            @pl.loop(0, CHUNKS)
            def _(c):
                for t in range(STEPS):
                    field[t][c, pl.ds(side * (CX + WIDTH), WIDTH)] = blank

        @pl.when(jnp.logical_not(has[1][side]))
        def _(side=side):
            @pl.loop(0, STEPS)
            def _(t):
                @pl.loop(0, CHUNKS)
                def _(c):
                    z_halo[side, t, c] = jnp.zeros((8, 8, 128), jnp.float32)

    def x_copy(t, c, way):
        return pltpu.make_async_remote_copy(
            src_ref=field[t].at[c, pl.ds(WIDTH + (1 - way) * (CX - WIDTH), WIDTH)],
            dst_ref=field[t].at[c, pl.ds(way * (CX + WIDTH), WIDTH)],
            send_sem=x_send.at[way, c],
            recv_sem=x_recv.at[way, t % 2, c],
            device_id={"slab": s + 1 - 2 * way},
            device_id_type=MESH,
        )

    def z_copy(t, c, way):
        return pltpu.make_async_remote_copy(
            src_ref=z_own.at[t, c, pl.ds(1, 8)],
            dst_ref=z_halo.at[way, t, c],
            send_sem=z_send.at[way, c],
            recv_sem=z_recv.at[way, t % 2, c],
            device_id={"grp": g + 1 - 2 * way},
            device_id_type=MESH,
        )

    def sending(axis, way):
        return has[axis][1 - way]

    def receiving(axis, way):
        return has[axis][way]

    pl.semaphore_wait(barrier, n_slab - 1 + n_x * (n_grp - 1))

    def pack(values):
        packed = jnp.zeros((8, 128), jnp.float32)
        for i, value in enumerate(values):
            packed = jnp.where(
                lane_slot == i, pltpu.roll(value, (4 + 8 * i) % 128, 1), packed
            )
        return packed

    def keep_parts(c, j, values):
        for i in range(0, 16, 2):
            high, low = split(jnp.concatenate(values[i : i + 2], axis=0))
            spot = pl.ds(pl.multiple_of(128 * j + 8 * i, 16), 16)
            parts_of[c, spot, pl.ds(0, 128)] = high
            parts_of[c, spot, pl.ds(128, 128)] = low

    def bring_in(c):
        loaded(c).wait()
        for way in range(2):

            @pl.when(sending(0, way))
            def _(way=way):
                x_copy(0, c, way).start()

        @pl.loop(0, CX // 2)
        def _(j):
            values = [field[0][c, WIDTH + 2 * j + i // 8, i % 8] for i in range(16)]
            z_own[0, c, j + 1] = pack(values)
            keep_parts(c, j, values)

        for way in range(2):

            @pl.when(sending(1, way))
            def _(way=way):
                z_copy(0, c, way).start()

    @pl.loop(0, GROUP)
    def _(c):
        bring_in(c)

    weights = jnp.zeros((1, 128), jnp.float32)
    for r in range(recs):
        weights = jnp.where(lane[:1] == r, weight[r], weights)

    def store(c, p):
        return pltpu.make_async_copy(
            field[STEPS].at[c, pl.ds(WIDTH, CX), :, p], wave_out.at[c * CHUNK + p], store_sem.at[c]
        )

    def advance(c, t):
        for way in range(2):

            @pl.when(receiving(0, way))
            def _(way=way):
                x_copy(t, c, way).wait_recv()

            @pl.when(receiving(1, way))
            def _(way=way):
                z_copy(t, c, way).wait_recv()

        left = z_halo[0, t, c].reshape(64, 128)
        right = z_halo[1, t, c].reshape(64, 128)
        half = lax.broadcasted_iota(jnp.int32, (64, 128), 1) % 8 < WIDTH
        high, low = split(jnp.where(half, left, right))
        both = jnp.dot(
            jnp.concatenate([high, low], axis=1), z_map[...], preferred_element_type=jnp.float32
        )
        z_fix[...] = (both[:, :128] + both[:, 128:]).reshape(8, 8, 128)
        before = max(t - 1, 0)
        both = jnp.dot(parts_of[c], z_band[...], preferred_element_type=jnp.float32)
        z_lap[...] = both[:, :128] + both[:, 128:]

        @pl.loop(0, CX // 2)
        def _(j):
            fix = z_fix[j]
            earlier = pl.multiple_of(16 * jnp.maximum(j - 1, 0), 16)

            if t < STEPS - 1:
                z_own[t + 1, c, j] = pack([latest[earlier + i] for i in range(16)])

            along_z = z_lap[pl.ds(pl.multiple_of(128 * j, 128), 128), :]
            values = []
            for i in range(16):
                y = i % 8
                x = 2 * j + i // 8

                def at(dx, dy):
                    return field[t][c, WIDTH + x + dx, y + dy]

                center = at(0, 0)
                total = along_z[8 * i : 8 * i + 8]
                for k in range(1, 5):
                    beside = at(k, 0) + at(-k, 0)
                    if y + k < CY:
                        beside = beside + at(0, k)
                    if y - k >= 0:
                        beside = beside + at(0, -k)
                    total = total + A[k] * beside
                correction = pltpu.roll(fix, (128 - 4 - 8 * i) % 128, 1)
                total = total + jnp.where(edge, correction, 0.0)
                old = field[before][c, WIDTH + x, y]
                value = (2.0 * center - old) + speed[x, y] * total
                field[t + 1][c, WIDTH + x, y] = value
                latest[16 * j + i] = value
                values.append(value)

            if t < STEPS - 1:
                keep_parts(c, j, values)

        if t < STEPS - 1:
            z_own[t + 1, c, 8] = pack([latest[112 + i] for i in range(16)])
            for way in range(2):

                @pl.when(sending(0, way))
                def _(way=way):
                    x_copy(t, c, way).wait_send()
                    x_copy(t + 1, c, way).start()

                @pl.when(sending(1, way))
                def _(way=way):
                    z_copy(t, c, way).wait_send()
                    z_copy(t + 1, c, way).start()

        if t == STEPS - 1:
            for way in range(2):

                @pl.when(sending(0, way))
                def _(way=way):
                    x_copy(t, c, way).wait_send()

                @pl.when(sending(1, way))
                def _(way=way):
                    z_copy(t, c, way).wait_send()

        found = jnp.zeros((8, 128), jnp.float32)
        for r in range(recs):
            value = pltpu.roll(latest[row_of[r]], turn_of[r], 1)
            found = jnp.where(lane == r, value, found)
        traces[t, pl.ds(c * CHUNK, CHUNK), :] = found * weights

        if t == STEPS - 1:
            for p in range(CHUNK):
                store(c, p).start()

    @pl.loop(0, CHUNKS // GROUP)
    def _(block):
        for t in range(STEPS):

            @pl.loop(0, GROUP)
            def _(k, t=t):
                c = block * GROUP + k
                advance(c, t)
                if t == STEPS - 1:

                    @pl.when(block < CHUNKS // GROUP - 1)
                    def _():
                        bring_in(c + GROUP)

    gram = jnp.zeros((PROBES, PROBES), jnp.float32)
    for t in range(STEPS):
        gram = gram + dot_nt(traces[t], traces[t])
    shares[...] = jnp.concatenate([gram, gram], axis=1).reshape(8, 8, 128)

    def push(k, count, me, source, target, stage, device):
        other = lax.rem(me + k, count)
        return pltpu.make_async_remote_copy(
            src_ref=source(other),
            dst_ref=target.at[me],
            send_sem=sum_send.at[stage],
            recv_sem=sum_recv.at[stage],
            device_id=device(other),
            device_id_type=MESH,
        )

    def arrived(buffer, count, sem):
        whole = buffer.at[pl.ds(0, count)]
        return pltpu.make_async_copy(whole, whole, sem)

    def added(buffer, count):
        total = buffer[0]
        for k in range(1, count):
            total = total + buffer[k]
        return total

    def in_row(other):
        return {"slab": place_x * n_y + other}

    def in_plane(other):
        return {"slab": other // n_grp * n_y + place_y, "grp": other % n_grp}

    sum_a[place_y] = shares[place_y]

    @pl.loop(1, n_y)
    def _(k):
        push(k, n_y, place_y, lambda other: shares.at[other], sum_a, 0, in_row).start()

    own_row = jnp.zeros((1, 128), jnp.int32)
    for r in range(recs):
        own_row = jnp.where(lane[:1] == r, owner[r], own_row)
    slot = jnp.zeros((1, 128), jnp.int32)
    for r in range(recs):
        slot = slot + jnp.where((own_row == owner[r]) & (lane[:1] > r), 1, 0)
    lane_row = lax.broadcasted_iota(jnp.int32, (1, 128), 1)
    target = jnp.where(lane_row < recs, own_row * CAP + slot, -1)
    spots = lax.broadcasted_iota(jnp.int32, (n_slab * CAP, 128), 0)
    placer = jnp.where(spots == target, 1.0, 0.0)
    outgoing[...] = dot_nt(placer, traces[...].reshape(STEPS * PROBES, 128)).reshape(
        n_slab, CAP, STEPS * PROBES
    )

    def to_owner(k):
        other = lax.rem(s + k, n_slab)
        return pltpu.make_async_remote_copy(
            src_ref=outgoing.at[other],
            dst_ref=incoming.at[s],
            send_sem=a2a_send,
            recv_sem=a2a_recv,
            device_id={"slab": other},
            device_id_type=MESH,
        )

    to_self = pltpu.make_async_copy(outgoing.at[s], incoming.at[s], own_sem)
    to_self.start()

    @pl.loop(1, n_slab)
    def _(k):
        to_owner(k).start()

    plane = n_x * n_grp
    place = place_x * n_grp + g
    arrived(sum_a, n_y - 1, sum_recv.at[0]).wait()
    sum_b[place] = added(sum_a, n_y)

    @pl.loop(1, plane)
    def _(k):
        push(k, plane, place, lambda other: sum_b.at[place], sum_b, 1, in_plane).start()

    arrived(sum_b, plane - 1, sum_recv.at[1]).wait()
    sum_c[place_y] = added(sum_b, plane)

    @pl.loop(1, n_y)
    def _(k):
        push(k, n_y, place_y, lambda other: sum_c.at[place_y], sum_c, 2, in_row).start()

    arrived(sum_c, n_y - 1, sum_recv.at[2]).wait()
    gram_out[...] = sum_c[...].reshape(PROBES, 128)

    arrived(shares, n_y - 1, sum_send.at[0]).wait()
    arrived(sum_b, plane - 1, sum_send.at[1]).wait()
    arrived(sum_c, n_y - 1, sum_send.at[2]).wait()
    to_self.wait()
    arrived(outgoing, n_slab - 1, a2a_send).wait()
    arrived(incoming, n_slab - 1, a2a_recv).wait()

    for c in range(CHUNKS):
        whole = field[STEPS].at[c, pl.ds(WIDTH, CX)]
        pltpu.make_async_copy(whole, whole, store_sem.at[c]).wait()


def finishing(count, wave_in, incoming, total, wave_out, q_out, r_out, held, sem):
    def chunk(ref, c):
        return ref.at[pl.ds(c * CHUNK, CHUNK)]

    into = [
        pltpu.make_async_copy(chunk(wave_in, c), held.at[c], sem.at[0, c]) for c in range(CHUNKS)
    ]
    back = [
        pltpu.make_async_copy(held.at[c], chunk(wave_out, c), sem.at[1, c]) for c in range(CHUNKS)
    ]
    for copy in into:
        copy.start()
    unit = lax.broadcasted_iota(jnp.int32, (PROBES, 128), 0)
    unit_lane = lax.broadcasted_iota(jnp.int32, (PROBES, 128), 1)
    work = jnp.where(
        unit_lane < PROBES, total[...], jnp.where(unit_lane - PROBES == unit, 1.0, 0.0)
    )
    parts = [work[8 * b : 8 * b + 8] for b in range(8)]
    sub = lax.broadcasted_iota(jnp.int32, (8, 128), 0)
    for k in range(PROBES):
        b0 = k // 8
        if k % 4 == 0 and 16 <= k < 16 + 4 * CHUNKS:
            into[k // 4 - 4].wait()
            back[k // 4 - 4].start()
        pivot_row = parts[b0][k % 8 : k % 8 + 1, :]
        scaled = pivot_row * (1.0 / pivot_row[:, k : k + 1])
        for b in range(b0, 8):
            factor = parts[b][:, k : k + 1]
            if b == b0:
                factor = jnp.where(sub > k % 8, factor, 0.0)
            parts[b] = parts[b] - factor * scaled
    work = jnp.concatenate(parts, axis=0)
    diag = jnp.sum(jnp.where(unit == unit_lane, work, 0.0), axis=1, keepdims=True)
    work = work * (1.0 / jnp.sqrt(diag))
    upper = jnp.where((unit_lane >= unit) & (unit_lane < PROBES), work, 0.0)
    r_out[...] = upper[:, :PROBES] * (1.0 / math.sqrt(count))
    inverse = jnp.where(unit_lane >= PROBES, work, 0.0) * math.sqrt(count)
    pair = jnp.concatenate([pltpu.roll(inverse, PROBES, 1), inverse], axis=0)
    for half in range(2):
        spot = pl.ds(128 * half, 128)
        q_out[:, spot] = dot_nt(incoming[:, spot], pair)
    for copy in back:
        copy.wait()


def solution(mesh):
    n_grp = mesh.shape["grp"]
    n_slab = mesh.shape["slab"]

    def per_device(probes, courant, rec_cell, rec_owner, trace_weight):
        recs = rec_cell.shape[0]
        f32 = jnp.float32
        smem = pl.BlockSpec(memory_space=pltpu.SMEM)
        vmem = pl.BlockSpec(memory_space=pltpu.VMEM)
        wave, incoming, total = pl.pallas_call(
            functools.partial(kernel, n_grp, n_slab),
            out_shape=(
                jax.ShapeDtypeStruct((PROBES, CX, CY, CZ), f32),
                jax.ShapeDtypeStruct((n_slab, CAP, STEPS * PROBES), f32),
                jax.ShapeDtypeStruct((PROBES, 128), f32),
            ),
            in_specs=[
                pl.BlockSpec(memory_space=pl.ANY),
                vmem,
                smem,
                smem,
                smem,
            ],
            out_specs=(pl.BlockSpec(memory_space=pl.ANY), vmem, vmem),
            scratch_shapes=[pltpu.VMEM((CHUNKS, CX + 2 * WIDTH, CY, CHUNK, CZ), f32)] * (STEPS + 1)
            + [
                pltpu.VMEM((CHUNKS, CX * CY * CHUNK, 2 * CZ), jnp.bfloat16),
                pltpu.VMEM((2 * CZ, 2 * CZ), jnp.bfloat16),
                pltpu.VMEM((CX * CY * CHUNK, CZ), f32),
                pltpu.SMEM((recs,), jnp.int32),
                pltpu.SMEM((recs,), jnp.int32),
                pltpu.VMEM((CX * CY, CHUNK, CZ), f32),
                pltpu.VMEM((CX, CY, 8, CZ), f32),
                pltpu.VMEM((STEPS, CHUNKS, 9, 8, 128), f32),
                pltpu.VMEM((2, STEPS, CHUNKS, 8, 8, 128), f32),
                pltpu.VMEM((8, 8, 128), f32),
                pltpu.VMEM((256, 256), jnp.bfloat16),
                pltpu.VMEM((STEPS, PROBES, 128), f32),
                pltpu.VMEM((n_slab, CAP, STEPS * PROBES), f32),
                pltpu.VMEM((8, 8, 128), f32),
                pltpu.VMEM((8, 8, 128), f32),
                pltpu.VMEM((n_slab // 8 * n_grp, 8, 128), f32),
                pltpu.VMEM((8, 8, 128), f32),
                pltpu.SemaphoreType.DMA((CHUNKS,)),
                pltpu.SemaphoreType.DMA((CHUNKS,)),
                pltpu.SemaphoreType.DMA((2, CHUNKS)),
                pltpu.SemaphoreType.DMA((2, 2, CHUNKS)),
                pltpu.SemaphoreType.DMA((2, CHUNKS)),
                pltpu.SemaphoreType.DMA((2, 2, CHUNKS)),
                pltpu.SemaphoreType.DMA,
                pltpu.SemaphoreType.DMA,
                pltpu.SemaphoreType.DMA,
                pltpu.SemaphoreType.DMA((3,)),
                pltpu.SemaphoreType.DMA((3,)),
            ],
            compiler_params=pltpu.CompilerParams(
                collective_id=0, has_side_effects=True, vmem_limit_bytes=56 * 1024 * 1024
            ),
        )(
            probes,
            courant,
            rec_cell,
            rec_owner.reshape(recs),
            trace_weight,
        )
        anywhere = pl.BlockSpec(memory_space=pl.ANY)
        return pl.pallas_call(
            functools.partial(finishing, n_slab * n_grp * recs * STEPS),
            out_shape=(
                jax.ShapeDtypeStruct((PROBES, CX, CY, CZ), f32),
                jax.ShapeDtypeStruct((n_slab * CAP, STEPS * PROBES), f32),
                jax.ShapeDtypeStruct((PROBES, PROBES), f32),
            ),
            in_specs=[anywhere, vmem, vmem],
            out_specs=(anywhere, vmem, vmem),
            scratch_shapes=[
                pltpu.VMEM((CHUNKS, CHUNK, CX, CY, CZ), f32),
                pltpu.SemaphoreType.DMA((2, CHUNKS)),
            ],
            compiler_params=pltpu.CompilerParams(vmem_limit_bytes=62 * 1024 * 1024),
        )(wave, incoming.reshape(n_slab * CAP, STEPS * PROBES), total)

    return jax.shard_map(
        per_device,
        mesh=mesh,
        in_specs=(
            P(None, "slab", None, "grp"),
            P("slab", None, "grp"),
            P(("grp", "slab")),
            P(("grp", "slab"), None),
            P(("grp", "slab")),
        ),
        out_specs=(P(None, "slab", None, "grp"), P(("grp", "slab"), None), P()),
        check_vma=False,
    )
```

```python
import functools
import math

import jax
import jax.numpy as jnp
from jax import lax
from jax.experimental import pallas as pl
from jax.experimental.pallas import tpu as pltpu
from jax.sharding import PartitionSpec as P
import numpy as np
import ml_dtypes

PROBES = 64
CX = 16
CY = 8
CZ = 128
STEPS = 4
CHUNK = 8
CHUNKS = PROBES // CHUNK
PAIR = 2
WIDTH = 4
CAP = 8
MESH = pl.DeviceIdType.MESH
EXACT = lax.Precision.HIGHEST

A0 = -205.0 / 72.0
A = (0.0, 8.0 / 5.0, -1.0 / 5.0, 8.0 / 315.0, -1.0 / 560.0)


def halves(value):
    high = float(np.float32(value).astype(ml_dtypes.bfloat16))
    low = float(np.float32(value - high).astype(ml_dtypes.bfloat16))
    return high, low


def banded(gap, low_part, coefficients):
    table = jnp.zeros(gap.shape, jnp.float32)
    for k, value in enumerate(coefficients):
        high, low = halves(value)
        table = jnp.where(gap == k, jnp.where(low_part, low, high), table)
    return table


def split(value):
    high = value.astype(jnp.bfloat16)
    low = (value - high.astype(jnp.float32)).astype(jnp.bfloat16)
    return high, low


def dot_nt(a, b):
    return lax.dot_general(
        a, b, (((1,), (1,)), ((), ())), precision=EXACT, preferred_element_type=jnp.float32
    )


def kernel(
    n_grp,
    n_slab,
    probes,
    courant,
    cell,
    owner,
    weight,
    wave_out,
    incoming,
    gram_out,
    field_0,
    field_1,
    field_2,
    field_3,
    field_4,
    parts_of,
    z_band,
    z_lap,
    row_of,
    turn_of,
    latest,
    speed,
    z_own,
    z_halo,
    z_fix,
    z_map,
    traces,
    outgoing,
    shares,
    sum_a,
    sum_b,
    sum_c,
    load_sem,
    store_sem,
    x_send,
    x_recv,
    z_send,
    z_recv,
    a2a_send,
    a2a_recv,
    own_sem,
    sum_send,
    sum_recv,
):
    field = (field_0, field_1, field_2, field_3, field_4)
    s = lax.axis_index("slab")
    g = lax.axis_index("grp")
    has = ((s > 0, s < n_slab - 1), (g > 0, g < n_grp - 1))

    def load(c, p):
        return pltpu.make_async_copy(
            probes.at[c * CHUNK + p], field[0].at[c, pl.ds(WIDTH, CX), :, p], load_sem.at[c]
        )

    def loaded(c):
        whole = field[0].at[c, pl.ds(WIDTH, CX)]
        return pltpu.make_async_copy(whole, whole, load_sem.at[c])

    for c in range(CHUNKS):
        for p in range(CHUNK):
            load(c, p).start()

    barrier = pltpu.get_barrier_semaphore()

    @pl.loop(1, n_slab)
    def _(k):
        pl.semaphore_signal(
            barrier, inc=1, device_id={"slab": lax.rem(s + k, n_slab)}, device_id_type=MESH
        )

    n_y = 8
    n_x = n_slab // n_y
    place_y = s % n_y
    place_x = s // n_y

    @pl.loop(n_x, n_x * n_grp)
    def _(k):
        pl.semaphore_signal(
            barrier,
            inc=1,
            device_id={
                "slab": lax.rem(place_x + k % n_x, n_x) * n_y + place_y,
                "grp": lax.rem(g + k // n_x, n_grp),
            },
            device_id_type=MESH,
        )

    lane = lax.broadcasted_iota(jnp.int32, (8, 128), 1)
    edge = (lane < WIDTH) | (lane >= CZ - WIDTH)
    lane_slot = lane // 8
    low_half = (lane % 8) < WIDTH

    row_i = lax.broadcasted_iota(jnp.int32, (256, 256), 0) % 128
    col_i = lax.broadcasted_iota(jnp.int32, (256, 256), 1)
    low_part = col_i >= 128
    col_i = col_i % 128
    gap = jnp.abs(row_i - col_i)
    crossing = (row_i // 8 == col_i // 8) & ((row_i % 8 < WIDTH) != (col_i % 8 < WIDTH))
    z_band[...] = banded(gap, low_part, (3.0 * A0,) + A[1:]).astype(jnp.bfloat16)
    z_map[...] = jnp.where(crossing, banded(gap, low_part, A), 0.0).astype(jnp.bfloat16)

    recs = cell.shape[0]

    @pl.loop(0, recs)
    def _(r):
        where = cell[r]
        row_of[r] = where // CZ
        turn_of[r] = (r + CZ - where % CZ) % CZ

    latest[...] = jnp.zeros(latest.shape, jnp.float32)

    @pl.loop(0, CX)
    def _(x):
        for y in range(CY):
            speed[x, y] = jnp.broadcast_to(courant[x, pl.ds(y, 1), :], (8, 128))

    blank = jnp.zeros((WIDTH, CY, 8, 128), jnp.float32)
    for side in range(2):

        @pl.when(jnp.logical_not(has[0][side]))
        def _(side=side):
            @pl.loop(0, CHUNKS)
            def _(c):
                for t in range(STEPS):
                    field[t][c, pl.ds(side * (CX + WIDTH), WIDTH)] = blank

        @pl.when(jnp.logical_not(has[1][side]))
        def _(side=side):
            @pl.loop(0, STEPS)
            def _(t):
                @pl.loop(0, CHUNKS)
                def _(c):
                    z_halo[side, t, c] = jnp.zeros((8, 8, 128), jnp.float32)

    def x_copy(t, c, way):
        return pltpu.make_async_remote_copy(
            src_ref=field[t].at[c, pl.ds(WIDTH + (1 - way) * (CX - WIDTH), WIDTH)],
            dst_ref=field[t].at[c, pl.ds(way * (CX + WIDTH), WIDTH)],
            send_sem=x_send.at[way, c],
            recv_sem=x_recv.at[way, t % 2, c],
            device_id={"slab": s + 1 - 2 * way},
            device_id_type=MESH,
        )

    def z_copy(t, c, way):
        return pltpu.make_async_remote_copy(
            src_ref=z_own.at[t, c, pl.ds(1, 8)],
            dst_ref=z_halo.at[way, t, c],
            send_sem=z_send.at[way, c],
            recv_sem=z_recv.at[way, t % 2, c],
            device_id={"grp": g + 1 - 2 * way},
            device_id_type=MESH,
        )

    def sending(axis, way):
        return has[axis][1 - way]

    def receiving(axis, way):
        return has[axis][way]

    pl.semaphore_wait(barrier, n_slab - 1 + n_x * (n_grp - 1))

    def pack(values):
        packed = jnp.zeros((8, 128), jnp.float32)
        for i, value in enumerate(values):
            packed = jnp.where(
                lane_slot == i, pltpu.roll(value, (4 + 8 * i) % 128, 1), packed
            )
        return packed

    def keep_parts(c, j, values):
        for i in range(0, 16, 2):
            high, low = split(jnp.concatenate(values[i : i + 2], axis=0))
            spot = pl.ds(pl.multiple_of(128 * j + 8 * i, 16), 16)
            parts_of[c, spot, pl.ds(0, 128)] = high
            parts_of[c, spot, pl.ds(128, 128)] = low

    def bring_in(c):
        loaded(c).wait()
        for way in range(2):

            @pl.when(sending(0, way))
            def _(way=way):
                x_copy(0, c, way).start()

        @pl.loop(0, CX // 2)
        def _(j):
            values = [field[0][c, WIDTH + 2 * j + i // 8, i % 8] for i in range(16)]
            z_own[0, c, j + 1] = pack(values)
            keep_parts(c, j, values)

        for way in range(2):

            @pl.when(sending(1, way))
            def _(way=way):
                z_copy(0, c, way).start()

    @pl.loop(0, CHUNKS)
    def _(c):
        bring_in(c)

    weights = jnp.zeros((1, 128), jnp.float32)
    for r in range(recs):
        weights = jnp.where(lane[:1] == r, weight[r], weights)

    def store(c, p):
        return pltpu.make_async_copy(
            field[STEPS].at[c, pl.ds(WIDTH, CX), :, p], wave_out.at[c * CHUNK + p], store_sem.at[c]
        )

    def advance(m, t):
        chunks = [PAIR * m + q for q in range(PAIR)]
        for c in chunks:
            for way in range(2):

                @pl.when(receiving(1, way))
                def _(c=c, way=way):
                    z_copy(t, c, way).wait_recv()

        here = pl.ds(PAIR * m, PAIR)
        left = z_halo[0, t, here].reshape(PAIR * 64, 128)
        right = z_halo[1, t, here].reshape(PAIR * 64, 128)
        half = lax.broadcasted_iota(jnp.int32, (PAIR * 64, 128), 1) % 8 < WIDTH
        high, low = split(jnp.where(half, left, right))
        both = jnp.dot(
            jnp.concatenate([high, low], axis=1), z_map[...], preferred_element_type=jnp.float32
        )
        z_fix[...] = (both[:, :128] + both[:, 128:]).reshape(PAIR * 8, 8, 128)
        before = max(t - 1, 0)
        rows = parts_of[here].reshape(PAIR * CX * CY * CHUNK, 2 * CZ)
        both = jnp.dot(rows, z_band[...], preferred_element_type=jnp.float32)
        z_lap[...] = both[:, :128] + both[:, 128:]

        def one_chunk(q, n):
            c = PAIR * m + q
            j = n - q * 8
            fix = z_fix[n]
            earlier = jnp.maximum(n - 1, 0)

            if t < STEPS - 1:
                z_own[t + 1, PAIR * m + earlier // 8, n - earlier // 8 * 8] = pack(
                    [latest[earlier * 16 + i] for i in range(16)]
                )

            along_z = z_lap[pl.ds(pl.multiple_of(128 * n, 128), 128), :]
            values = []
            for i in range(16):
                y = i % 8
                x = 2 * j + i // 8

                def at(dx, dy):
                    return field[t][c, WIDTH + x + dx, y + dy]

                center = at(0, 0)
                total = along_z[8 * i : 8 * i + 8]
                for k in range(1, 5):
                    beside = at(k, 0) + at(-k, 0)
                    if y + k < CY:
                        beside = beside + at(0, k)
                    if y - k >= 0:
                        beside = beside + at(0, -k)
                    total = total + A[k] * beside
                correction = pltpu.roll(fix, (128 - 4 - 8 * i) % 128, 1)
                total = total + jnp.where(edge, correction, 0.0)
                old = field[before][c, WIDTH + x, y]
                value = (2.0 * center - old) + speed[x, y] * total
                field[t + 1][c, WIDTH + x, y] = value
                latest[16 * n + i] = value
                values.append(value)

            if t < STEPS - 1:
                keep_parts(c, j, values)

        for q, c in enumerate(chunks):
            for way in range(2):

                @pl.when(receiving(0, way))
                def _(c=c, way=way):
                    x_copy(t, c, way).wait_recv()

            pl.loop(8 * q, 8 * q + 8)(functools.partial(one_chunk, q))
            for way in range(2):

                @pl.when(sending(0, way))
                def _(c=c, way=way):
                    x_copy(t, c, way).wait_send()
                    if t < STEPS - 1:
                        x_copy(t + 1, c, way).start()

        if t < STEPS - 1:
            z_own[t + 1, PAIR * m + PAIR - 1, 8] = pack(
                [latest[PAIR * 128 - 16 + i] for i in range(16)]
            )
        for c in chunks:
            for way in range(2):

                @pl.when(sending(1, way))
                def _(c=c, way=way):
                    z_copy(t, c, way).wait_send()
                    if t < STEPS - 1:
                        z_copy(t + 1, c, way).start()

        found = [jnp.zeros((8, 128), jnp.float32) for _ in chunks]
        for r in range(recs):
            row, turn = row_of[r], turn_of[r]
            for q in range(PAIR):
                value = pltpu.roll(latest[q * CX * CY + row], turn, 1)
                found[q] = jnp.where(lane == r, value, found[q])
        for c, value in zip(chunks, found):
            traces[t, pl.ds(c * CHUNK, CHUNK), :] = value * weights

        if t == STEPS - 1:
            for c in chunks:
                for p in range(CHUNK):
                    store(c, p).start()

    for t in range(STEPS):

        @pl.loop(0, CHUNKS // PAIR)
        def _(m, t=t):
            advance(m, t)

    gram = jnp.zeros((PROBES, PROBES), jnp.float32)
    for t in range(STEPS):
        gram = gram + dot_nt(traces[t], traces[t])
    shares[...] = jnp.concatenate([gram, gram], axis=1).reshape(8, 8, 128)

    def push(k, count, me, source, target, stage, device):
        other = lax.rem(me + k, count)
        return pltpu.make_async_remote_copy(
            src_ref=source(other),
            dst_ref=target.at[me],
            send_sem=sum_send.at[stage],
            recv_sem=sum_recv.at[stage],
            device_id=device(other),
            device_id_type=MESH,
        )

    def arrived(buffer, count, sem):
        whole = buffer.at[pl.ds(0, count)]
        return pltpu.make_async_copy(whole, whole, sem)

    def added(buffer, count):
        total = buffer[0]
        for k in range(1, count):
            total = total + buffer[k]
        return total

    def in_row(other):
        return {"slab": place_x * n_y + other}

    def in_plane(other):
        return {"slab": other // n_grp * n_y + place_y, "grp": other % n_grp}

    sum_a[place_y] = shares[place_y]

    @pl.loop(1, n_y)
    def _(k):
        push(k, n_y, place_y, lambda other: shares.at[other], sum_a, 0, in_row).start()

    own_row = jnp.zeros((1, 128), jnp.int32)
    for r in range(recs):
        own_row = jnp.where(lane[:1] == r, owner[r], own_row)
    slot = jnp.zeros((1, 128), jnp.int32)
    for r in range(recs):
        slot = slot + jnp.where((own_row == owner[r]) & (lane[:1] > r), 1, 0)
    lane_row = lax.broadcasted_iota(jnp.int32, (1, 128), 1)
    target = jnp.where(lane_row < recs, own_row * CAP + slot, -1)
    spots = lax.broadcasted_iota(jnp.int32, (n_slab * CAP, 128), 0)
    placer = jnp.where(spots == target, 1.0, 0.0)
    outgoing[...] = dot_nt(placer, traces[...].reshape(STEPS * PROBES, 128)).reshape(
        n_slab, CAP, STEPS * PROBES
    )

    def to_owner(k):
        other = lax.rem(s + k, n_slab)
        return pltpu.make_async_remote_copy(
            src_ref=outgoing.at[other],
            dst_ref=incoming.at[s],
            send_sem=a2a_send,
            recv_sem=a2a_recv,
            device_id={"slab": other},
            device_id_type=MESH,
        )

    to_self = pltpu.make_async_copy(outgoing.at[s], incoming.at[s], own_sem)
    to_self.start()

    @pl.loop(1, n_slab)
    def _(k):
        to_owner(k).start()

    plane = n_x * n_grp
    place = place_x * n_grp + g
    arrived(sum_a, n_y - 1, sum_recv.at[0]).wait()
    sum_b[place] = added(sum_a, n_y)

    @pl.loop(1, plane)
    def _(k):
        push(k, plane, place, lambda other: sum_b.at[place], sum_b, 1, in_plane).start()

    arrived(sum_b, plane - 1, sum_recv.at[1]).wait()
    sum_c[place_y] = added(sum_b, plane)

    @pl.loop(1, n_y)
    def _(k):
        push(k, n_y, place_y, lambda other: sum_c.at[place_y], sum_c, 2, in_row).start()

    arrived(sum_c, n_y - 1, sum_recv.at[2]).wait()
    gram_out[...] = sum_c[...].reshape(PROBES, 128)

    arrived(shares, n_y - 1, sum_send.at[0]).wait()
    arrived(sum_b, plane - 1, sum_send.at[1]).wait()
    arrived(sum_c, n_y - 1, sum_send.at[2]).wait()
    to_self.wait()
    arrived(outgoing, n_slab - 1, a2a_send).wait()
    arrived(incoming, n_slab - 1, a2a_recv).wait()

    for c in range(CHUNKS):
        whole = field[STEPS].at[c, pl.ds(WIDTH, CX)]
        pltpu.make_async_copy(whole, whole, store_sem.at[c]).wait()


def finishing(count, wave_in, incoming, total, wave_out, q_out, r_out, held, sem):
    def chunk(ref, c):
        return ref.at[pl.ds(c * CHUNK, CHUNK)]

    into = [
        pltpu.make_async_copy(chunk(wave_in, c), held.at[c], sem.at[0, c]) for c in range(CHUNKS)
    ]
    back = [
        pltpu.make_async_copy(held.at[c], chunk(wave_out, c), sem.at[1, c]) for c in range(CHUNKS)
    ]
    for copy in into:
        copy.start()
    unit = lax.broadcasted_iota(jnp.int32, (PROBES, 128), 0)
    unit_lane = lax.broadcasted_iota(jnp.int32, (PROBES, 128), 1)
    work = jnp.where(
        unit_lane < PROBES, total[...], jnp.where(unit_lane - PROBES == unit, 1.0, 0.0)
    )
    parts = [work[8 * b : 8 * b + 8] for b in range(8)]
    sub = lax.broadcasted_iota(jnp.int32, (8, 128), 0)
    for k in range(PROBES):
        b0 = k // 8
        if k % 4 == 0 and 16 <= k < 16 + 4 * CHUNKS:
            into[k // 4 - 4].wait()
            back[k // 4 - 4].start()
        pivot_row = parts[b0][k % 8 : k % 8 + 1, :]
        scaled = pivot_row * (1.0 / pivot_row[:, k : k + 1])
        for b in range(b0, 8):
            factor = parts[b][:, k : k + 1]
            if b == b0:
                factor = jnp.where(sub > k % 8, factor, 0.0)
            parts[b] = parts[b] - factor * scaled
    work = jnp.concatenate(parts, axis=0)
    diag = jnp.sum(jnp.where(unit == unit_lane, work, 0.0), axis=1, keepdims=True)
    work = work * (1.0 / jnp.sqrt(diag))
    upper = jnp.where((unit_lane >= unit) & (unit_lane < PROBES), work, 0.0)
    r_out[...] = upper[:, :PROBES] * (1.0 / math.sqrt(count))
    inverse = jnp.where(unit_lane >= PROBES, work, 0.0) * math.sqrt(count)
    pair = jnp.concatenate([pltpu.roll(inverse, PROBES, 1), inverse], axis=0)
    for half in range(2):
        spot = pl.ds(128 * half, 128)
        q_out[:, spot] = dot_nt(incoming[:, spot], pair)
    for copy in back:
        copy.wait()


def solution(mesh):
    n_grp = mesh.shape["grp"]
    n_slab = mesh.shape["slab"]

    def per_device(probes, courant, rec_cell, rec_owner, trace_weight):
        recs = rec_cell.shape[0]
        f32 = jnp.float32
        smem = pl.BlockSpec(memory_space=pltpu.SMEM)
        vmem = pl.BlockSpec(memory_space=pltpu.VMEM)
        wave, incoming, total = pl.pallas_call(
            functools.partial(kernel, n_grp, n_slab),
            out_shape=(
                jax.ShapeDtypeStruct((PROBES, CX, CY, CZ), f32),
                jax.ShapeDtypeStruct((n_slab, CAP, STEPS * PROBES), f32),
                jax.ShapeDtypeStruct((PROBES, 128), f32),
            ),
            in_specs=[
                pl.BlockSpec(memory_space=pl.ANY),
                vmem,
                smem,
                smem,
                smem,
            ],
            out_specs=(pl.BlockSpec(memory_space=pl.ANY), vmem, vmem),
            scratch_shapes=[pltpu.VMEM((CHUNKS, CX + 2 * WIDTH, CY, CHUNK, CZ), f32)] * (STEPS + 1)
            + [
                pltpu.VMEM((CHUNKS, CX * CY * CHUNK, 2 * CZ), jnp.bfloat16),
                pltpu.VMEM((2 * CZ, 2 * CZ), jnp.bfloat16),
                pltpu.VMEM((PAIR * CX * CY * CHUNK, CZ), f32),
                pltpu.SMEM((recs,), jnp.int32),
                pltpu.SMEM((recs,), jnp.int32),
                pltpu.VMEM((PAIR * CX * CY, CHUNK, CZ), f32),
                pltpu.VMEM((CX, CY, 8, CZ), f32),
                pltpu.VMEM((STEPS, CHUNKS, 9, 8, 128), f32),
                pltpu.VMEM((2, STEPS, CHUNKS, 8, 8, 128), f32),
                pltpu.VMEM((PAIR * 8, 8, 128), f32),
                pltpu.VMEM((256, 256), jnp.bfloat16),
                pltpu.VMEM((STEPS, PROBES, 128), f32),
                pltpu.VMEM((n_slab, CAP, STEPS * PROBES), f32),
                pltpu.VMEM((8, 8, 128), f32),
                pltpu.VMEM((8, 8, 128), f32),
                pltpu.VMEM((n_slab // 8 * n_grp, 8, 128), f32),
                pltpu.VMEM((8, 8, 128), f32),
                pltpu.SemaphoreType.DMA((CHUNKS,)),
                pltpu.SemaphoreType.DMA((CHUNKS,)),
                pltpu.SemaphoreType.DMA((2, CHUNKS)),
                pltpu.SemaphoreType.DMA((2, 2, CHUNKS)),
                pltpu.SemaphoreType.DMA((2, CHUNKS)),
                pltpu.SemaphoreType.DMA((2, 2, CHUNKS)),
                pltpu.SemaphoreType.DMA,
                pltpu.SemaphoreType.DMA,
                pltpu.SemaphoreType.DMA,
                pltpu.SemaphoreType.DMA((3,)),
                pltpu.SemaphoreType.DMA((3,)),
            ],
            compiler_params=pltpu.CompilerParams(
                collective_id=0, has_side_effects=True, vmem_limit_bytes=56 * 1024 * 1024
            ),
        )(
            probes,
            courant,
            rec_cell,
            rec_owner.reshape(recs),
            trace_weight,
        )
        anywhere = pl.BlockSpec(memory_space=pl.ANY)
        return pl.pallas_call(
            functools.partial(finishing, n_slab * n_grp * recs * STEPS),
            out_shape=(
                jax.ShapeDtypeStruct((PROBES, CX, CY, CZ), f32),
                jax.ShapeDtypeStruct((n_slab * CAP, STEPS * PROBES), f32),
                jax.ShapeDtypeStruct((PROBES, PROBES), f32),
            ),
            in_specs=[anywhere, vmem, vmem],
            out_specs=(anywhere, vmem, vmem),
            scratch_shapes=[
                pltpu.VMEM((CHUNKS, CHUNK, CX, CY, CZ), f32),
                pltpu.SemaphoreType.DMA((2, CHUNKS)),
            ],
            compiler_params=pltpu.CompilerParams(vmem_limit_bytes=62 * 1024 * 1024),
        )(wave, incoming.reshape(n_slab * CAP, STEPS * PROBES), total)

    return jax.shard_map(
        per_device,
        mesh=mesh,
        in_specs=(
            P(None, "slab", None, "grp"),
            P("slab", None, "grp"),
            P(("grp", "slab")),
            P(("grp", "slab"), None),
            P(("grp", "slab")),
        ),
        out_specs=(P(None, "slab", None, "grp"), P(("grp", "slab"), None), P()),
        check_vma=False,
    )
```
